32 devices in a mesh: expert: 8 (over z, y), replica: 4 (over x, core).
Axes of the slice: x: 2, y: 2, z: 4, core: 2. Of those that a mesh axis runs over, the one named last changes fastest.
Arguments:
- tokens: bfloat16 [4096, 2048], P(('expert', 'replica')), may hold values from -6 to 6
- expert_ids: int32 [4096, 8], P(('expert', 'replica')), may hold values from 0 to 31, as said below
- gates: float32 [4096, 8], P(('expert', 'replica')), may hold values from 0.02 to 0.25
- cotangent: bfloat16 [4096, 2048], P(('expert', 'replica')), may hold values from -6 to 6
- expert_weights: bfloat16 [32, 2048, 1152], P(('expert', 'replica')), may hold values from -0.125 to 0.125
- moment_first: bfloat16 [32, 2048, 1152], P(('expert', 'replica')), may hold values from -0.00021362305 to 0.00021362305
- moment_second: bfloat16 [32, 2048, 1152], P(('expert', 'replica')), may hold values from 1.3242243e-09 to 1.3213139e-08
- hot_slot: int32 [8], P('expert'), may hold values from 0 to 3
Outputs:
- mixed: bfloat16 [4096, 2048], P(('expert', 'replica'))
- input_grad: bfloat16 [4096, 2048], P(('expert', 'replica'))
- gate_grad: float32 [4096, 8], P(('expert', 'replica'))
- new_weights: bfloat16 [32, 2048, 1152], P(('expert', 'replica'))
- hot_copy: bfloat16 [32, 2048, 1152], P(('expert', 'replica'))
The draws below stay inside these ranges and needn't reach their ends.
Inputs may be any that keep to these rules, and one draw needn't show every extreme that they name: `expert_ids`: each token names 8 different experts. Experts form 8 groups of 4 consecutive numbers. Of the choices of the 128 tokens of one device (aligned blocks of rows), exactly 128 name experts of each group; in group a the expert a * 4 + hot_slot[a] is named exactly 64 times, every other expert at most 32 times, and one of them exactly 32 times.
All inputs are finite; a program needn't handle non-finite values.
Results may differ from the reference program's by a relative error of at most 0.011.
Values may be sent and summed in bfloat16 or wider, within the bound.
No kernel may reach another device: no remote copies, remote signals or barrier semaphores. Data moves between devices by JAX's collectives and lax.ppermute only.
A program may use at most 256 MiB of HBM per device.

```python
import math
import jax
import jax.numpy as jnp
from jax import lax

D = 2048
F = 384
TOP = 8
TOK_DEV = 128
EXPERTS = 32
GROUPS = 8
TOKENS = 4096
CAP = 64
HALF = 32


def draw_routing(key):
    members = EXPERTS // GROUPS
    hot_member = jax.random.randint(jax.random.fold_in(key, 11), (GROUPS,), 0, members).astype(jnp.int32)
    full_rel = jax.random.randint(jax.random.fold_in(key, 12), (EXPERTS, GROUPS), 1, members).astype(jnp.int32)
    split_keys = jax.random.split(jax.random.fold_in(key, 13), EXPERTS * GROUPS)

    def first_share(one_key):
        shuffled = jax.random.permutation(one_key, 2 * HALF)
        return jnp.sum((shuffled[:HALF] < HALF).astype(jnp.int32))
    share = jax.vmap(first_share)(split_keys).reshape(EXPERTS, GROUPS)
    first_other = jnp.where(full_rel == 1, 2, 1)
    relative = jnp.arange(members, dtype=jnp.int32)[None, None, :]
    counts_rel = jnp.where(relative == 0, CAP, jnp.where(relative == full_rel[:, :, None], HALF, jnp.where(relative == first_other[:, :, None], share[:, :, None], HALF - share[:, :, None])))
    member_rel = (jnp.arange(members, dtype=jnp.int32)[None, :] - hot_member[:, None]) % members
    counts = jnp.take_along_axis(counts_rel, jnp.broadcast_to(member_rel[None], (EXPERTS, GROUPS, members)), axis=2).reshape(EXPERTS, EXPERTS)
    ends = jnp.cumsum(counts, axis=1)
    places = jnp.arange(TOK_DEV * TOP, dtype=jnp.int32)

    def list_block(row_ends):
        return jnp.searchsorted(row_ends, places, side='right')
    listed = jax.vmap(list_block)(ends).astype(jnp.int32)
    chosen = listed.reshape(EXPERTS, TOP, TOK_DEV).transpose(0, 2, 1)
    row_keys = jax.random.split(jax.random.fold_in(key, 14), EXPERTS)

    def shuffle_rows(one_key):
        return jax.random.permutation(one_key, TOK_DEV)
    row_order = jax.vmap(shuffle_rows)(row_keys)
    chosen = jnp.take_along_axis(chosen, row_order[:, :, None], axis=1)
    scores = jax.random.randint(jax.random.fold_in(key, 15), (EXPERTS, TOK_DEV, TOP), 0, 1 << 20) * TOP + jnp.arange(TOP, dtype=jnp.int32)[None, None, :]
    column_order = jnp.argsort(scores, axis=2)
    chosen = jnp.take_along_axis(chosen, column_order, axis=2)
    return (chosen.reshape(EXPERTS * TOK_DEV, TOP).astype(jnp.int32), hot_member)


def draw_expert_ids(key, part):
    return draw_routing(key)[0]


def draw_hot_slot(key, part):
    return draw_routing(key)[1]


def levels(key, shape, shards, least, largest):
    level, own = 1.0, jax.random.fold_in(key, 6)
    for position, parts in shards:
        steps = jnp.exp(jax.random.uniform(jax.random.fold_in(own, position), (parts,), jnp.float32, least / len(shards), largest / len(shards)))
        level = level * jnp.repeat(steps, shape[position] // parts).reshape([-1 if axis == position else 1 for axis in range(len(shape))])
    return level


def gaussian(rng, extent, width, reach, cuts=(), kind=jnp.bfloat16):
    result = width * jax.random.normal(rng, extent, jnp.float32)
    if cuts:
        result = result * levels(rng, extent, cuts, -0.22, 0.18)
    return jnp.clip(result, -reach, reach).astype(kind)


def setup_inputs(seed: int = 0) -> dict:
    keys = jax.random.split(jax.random.key(seed), 9)
    return {
        "tokens": gaussian(keys[0], (TOKENS, D), 1.0, 6.0, ((0, 32),)),
        "expert_ids": draw_expert_ids(jax.random.fold_in(keys[8], 71), 0),
        "gates": jnp.clip(0.02 + 0.23 * jax.random.uniform(keys[2], (TOKENS, TOP), jnp.float32) ** levels(keys[2], (TOKENS, TOP), ((0, 32),), -0.2, 0.2), 0.02, 0.25),
        "cotangent": gaussian(keys[3], (TOKENS, D), 1.0, 6.0, ((0, 32),)),
        "expert_weights": gaussian(keys[4], (EXPERTS, D, 3 * F), D ** -0.5, 0.125, ((0, 32),)),
        "moment_first": gaussian(keys[5], (EXPERTS, D, 3 * F), (0.3 / (3 * EXPERTS * D * F) ** 0.5), 0.00021362305, ((0, 32),)),
        "moment_second": jnp.clip(jnp.exp(math.log(1.3213139027357101e-08) - 2.30038487 * jax.random.uniform(keys[6], (EXPERTS, D, 3 * F), jnp.float32) ** levels(keys[6], (EXPERTS, D, 3 * F), ((0, 32),), -0.2, 0.2)), 1.3242242857813835e-09, 1.3213139027357101e-08).astype(jnp.bfloat16),
        "hot_slot": draw_hot_slot(jax.random.fold_in(keys[8], 71), 0),
    }


beta_first = 0.9
beta_second = 0.95
adam_eps = 1e-08
rate = 0.05
clip_norm = 1.0
bias_first = 1.0 - 0.9 ** 10
bias_second = 1.0 - 0.95 ** 10

def forward_rows(row_block, weights, hidden_width):
    gate_up = jnp.dot(row_block, weights[:, :2 * hidden_width], preferred_element_type=jnp.float32)
    gate_in = gate_up[:, :hidden_width]
    up_part = gate_up[:, hidden_width:]
    hidden = (gate_in * jax.nn.sigmoid(gate_in) * up_part).astype(jnp.bfloat16)
    outputs = jnp.dot(hidden, weights[:, 2 * hidden_width:].T, preferred_element_type=jnp.float32).astype(jnp.bfloat16)
    return (outputs, gate_up, hidden)

def backward_rows(cot_block, gate_up, weights, hidden_width):
    gate_in = gate_up[:, :hidden_width]
    up_part = gate_up[:, hidden_width:]
    sigmoid_gate = jax.nn.sigmoid(gate_in)
    hidden_grad = jnp.dot(cot_block, weights[:, 2 * hidden_width:], preferred_element_type=jnp.float32)
    grad_gate = hidden_grad * up_part * sigmoid_gate * (1.0 + gate_in * (1.0 - sigmoid_gate))
    grad_up = hidden_grad * gate_in * sigmoid_gate
    input_both = jnp.concatenate([grad_gate, grad_up], axis=1).astype(jnp.bfloat16)
    slot_grads = jnp.dot(input_both, weights[:, :2 * hidden_width].T, preferred_element_type=jnp.float32).astype(jnp.bfloat16)
    return (slot_grads, input_both)

def reference(tokens, expert_ids, gates, cotangent, expert_weights, moment_first, moment_second, hot_slot):
    hidden_width = F
    members = EXPERTS // GROUPS
    slot_total = TOK_DEV * TOP
    blocks = expert_ids.reshape(EXPERTS, slot_total)
    gate_flat = gates.reshape(-1)
    block_index = jnp.arange(EXPERTS, dtype=jnp.int32)
    slot_range = jnp.broadcast_to(jnp.arange(slot_total, dtype=jnp.int32)[None, :], (EXPERTS, slot_total))
    shape_four = (GROUPS, members, CAP, -1)
    clip_bound = clip_norm * EXPERTS ** (-0.5)

    def one_expert(carry, expert):
        mixed_acc, input_acc, gate_acc = carry
        matched = blocks == expert
        order_in = jnp.cumsum(matched.astype(jnp.int32), axis=1) - 1
        target = jnp.where(matched, order_in, CAP).astype(jnp.int32)
        table = jnp.zeros((EXPERTS, CAP + 1), jnp.int32).at[block_index[:, None], target].set(slot_range)[:, :CAP]
        counts = lax.optimization_barrier(jnp.sum(matched.astype(jnp.int32), axis=1))
        valid = (jnp.arange(CAP, dtype=jnp.int32)[None, :] < counts[:, None]).reshape(-1)
        slot_id = (table + block_index[:, None] * slot_total).reshape(-1).astype(jnp.int32)
        token_id = (slot_id // TOP).astype(jnp.int32)
        weights = expert_weights[expert]
        row_block = jnp.where(valid[:, None], tokens[token_id], jnp.zeros((), jnp.bfloat16))
        slot_gate = jnp.where(valid, gate_flat[slot_id], jnp.zeros((), jnp.float32))
        cot_rows = cotangent[token_id].astype(jnp.float32)
        cot_block = (slot_gate[:, None] * cot_rows).astype(jnp.bfloat16)
        outputs, gate_up, hidden = forward_rows(row_block, weights, hidden_width)
        out_wide = outputs.astype(jnp.float32)
        mixed_acc = mixed_acc.at[token_id].add(slot_gate[:, None] * out_wide)
        gate_acc = gate_acc.at[slot_id].add(jnp.where(valid, lax.optimization_barrier(jnp.sum(cot_rows * out_wide, axis=1)), jnp.zeros((), jnp.float32)))
        slot_grads, input_both = backward_rows(cot_block, gate_up, weights, hidden_width)
        input_acc = input_acc.at[token_id].add(slot_grads.astype(jnp.float32))
        in_part = jnp.einsum('arcd,arcg->rdg', row_block.astype(jnp.float32).reshape(shape_four), input_both.astype(jnp.float32).reshape(shape_four))
        down_part = jnp.einsum('arcd,arcf->rdf', cot_block.astype(jnp.float32).reshape(shape_four), hidden.astype(jnp.float32).reshape(shape_four))
        partial_value = lax.optimization_barrier(jnp.concatenate([in_part, down_part], axis=2).astype(jnp.bfloat16))
        gradient = lax.optimization_barrier(jnp.sum(partial_value.astype(jnp.float32), axis=0))
        return ((mixed_acc, input_acc, gate_acc), gradient)
    start = (jnp.zeros((TOKENS, D), jnp.float32), jnp.zeros((TOKENS, D), jnp.float32), jnp.zeros((TOKENS * TOP,), jnp.float32))
    carry, gradients = lax.scan(one_expert, start, jnp.arange(EXPERTS, dtype=jnp.int32))

    def adam_one(packed):
        gradient, weights, first_in, second_in = packed
        scale = jnp.minimum(1.0, clip_bound / (jnp.sqrt(jnp.sum(gradient * gradient)) + 1e-06))
        scaled = scale * gradient
        first = beta_first * first_in.astype(jnp.float32) + (1.0 - beta_first) * scaled
        second = beta_second * second_in.astype(jnp.float32) + (1.0 - beta_second) * scaled * scaled
        update = first / bias_first / (jnp.sqrt(second / bias_second) + adam_eps)
        return (weights.astype(jnp.float32) - rate * update).astype(jnp.bfloat16)
    new_weights = lax.map(adam_one, (gradients, expert_weights, moment_first, moment_second))
    owner = jnp.arange(EXPERTS, dtype=jnp.int32) // members
    hot_copy = new_weights[owner * members + hot_slot[owner]]
    return (carry[0].astype(jnp.bfloat16), carry[1].astype(jnp.bfloat16), carry[2].reshape(TOKENS, TOP), new_weights, hot_copy)
```

```python
import jax
import jax.numpy as jnp
from jax import lax
from jax.sharding import PartitionSpec as P

beta_first = 0.9
beta_second = 0.95
adam_eps = 1e-08
rate = 0.05
clip_norm = 1.0
bias_first = 1.0 - 0.9**10
bias_second = 1.0 - 0.95**10
BOTH = ("expert", "replica")
F32 = jnp.float32
BF16 = jnp.bfloat16


class Grid:
    def __init__(self, groups, owners):
        self.line = groups // 2
        self.sides = owners // 2
        self.owners = owners
        self.count = groups * owners

    def split(self, device):
        place, owner = device // self.owners, device % self.owners
        return place // 2, place % 2, owner // 2, owner % 2

    def join(self, line, row, side, core):
        return ((line * 2 + row) * self.sides + side) * 2 + core

    def move(self, value, step):
        pairs = [(d, self.join(*step(*self.split(d)))) for d in range(self.count)]
        return lax.ppermute(value, BOTH, pairs)

    def up(self, value):
        return self.move(value, lambda z, y, x, c: ((z + 1) % self.line, y, x, c))

    def down(self, value):
        return self.move(value, lambda z, y, x, c: ((z - 1) % self.line, y, x, c))

    def cross_a(self, value):
        return self.move(value, lambda z, y, x, c: (z, y ^ (1 - c), x ^ c, c))

    def cross_b(self, value):
        return self.move(value, lambda z, y, x, c: (z, y ^ c, x ^ (1 - c), c))

    def cross_side(self, value):
        return self.move(value, lambda z, y, x, c: (z, y, x ^ 1, c))

    def cross_core(self, value):
        return self.move(value, lambda z, y, x, c: (z, y, x, c ^ 1))


def chunk_compute(slots, select, row_gate, weights, width):
    blocks, room, token_count = select.shape[1:]
    stacked = jnp.stack(slots)
    rows = jnp.einsum(
        "eqjt,qtd->eqjd", select, stacked[:, :token_count], preferred_element_type=BF16
    )
    cots = jnp.einsum(
        "eqjt,qtd->eqjd", select, stacked[:, token_count:], preferred_element_type=BF16
    )
    kept, mixed, dx, grads = [], [], [], []
    for e in range(2):
        row_e = rows[e].reshape(blocks * room, -1)
        cot_e = cots[e].reshape(blocks * room, -1)
        gate = row_gate[e].reshape(blocks * room, 1)
        gate_up = jnp.dot(row_e, weights[e][:, : 2 * width], preferred_element_type=F32)
        spread = jnp.dot(cot_e, weights[e][:, 2 * width :], preferred_element_type=F32)
        gate_in, up_in = gate_up[:, :width], gate_up[:, width:]
        sig = jax.nn.sigmoid(gate_in)
        hidden = gate_in * sig * up_in
        grads.append(jnp.sum(hidden * spread, axis=1).reshape(blocks, room))
        hidden_gated = (hidden * gate).astype(BF16)
        hidden_grad = spread * gate
        both = jnp.concatenate(
            [hidden_grad * up_in * sig * (1.0 + gate_in * (1.0 - sig)), hidden_grad * gate_in * sig],
            axis=1,
        ).astype(BF16)
        nt = (((1,), (1,)), ((), ()))
        mixed.append(
            lax.dot_general(
                hidden_gated, weights[e][:, 2 * width :], nt, preferred_element_type=F32
            ).astype(BF16)
        )
        dx.append(
            lax.dot_general(
                both, weights[e][:, : 2 * width], nt, preferred_element_type=F32
            ).astype(BF16)
        )
        kept.append((row_e, cot_e, both, hidden_gated))
    mixed = jnp.stack(mixed).reshape(2, blocks, room, -1)
    dx = jnp.stack(dx).reshape(2, blocks, room, -1)
    mixed_part = jnp.einsum("eqjt,eqjd->qtd", select, mixed, preferred_element_type=F32)
    dx_part = jnp.einsum("eqjt,eqjd->qtd", select, dx, preferred_element_type=F32)
    parts = jnp.concatenate([mixed_part, dx_part], axis=1).astype(BF16)
    return [parts[q] for q in range(blocks)], kept, jnp.stack(grads)


def add(*values):
    total = values[0].astype(F32)
    for value in values[1:]:
        total = total + value.astype(F32)
    return total


def shards(
    tokens, expert_ids, gates, cotangent, expert_weights, moment_first, moment_second, hot_slot
):
    groups = lax.axis_size("expert")
    owners = lax.axis_size("replica")
    experts = groups * owners
    grid = Grid(groups, owners)
    line = grid.line
    token_count, chosen = expert_ids.shape
    width = expert_weights.shape[2] // 3
    room = 2 * token_count * chosen // experts
    device = lax.axis_index("expert") * owners + lax.axis_index("replica")
    z, y, x, c = grid.split(device)
    weights = expert_weights[0]

    expert_range = jnp.arange(experts, dtype=jnp.int32)
    hit = expert_ids[:, :, None] == expert_range
    gate_table = jnp.sum(jnp.where(hit, gates[:, :, None], 0.0), axis=1).T
    by_chip = gate_table.reshape(experts // 2, 1, 2, token_count)
    send = jnp.broadcast_to(by_chip, (experts // 2, 2, 2, token_count))
    table = lax.all_to_all(
        send.reshape(experts, 2 * token_count), BOTH, split_axis=0, concat_axis=0, tiled=True
    ).reshape(experts, 2, token_count)
    steps = jnp.arange(line, dtype=jnp.int32)[:, None]
    flip_a = jnp.array([0, 1, 0, 1], jnp.int32)[None]
    flip_b = jnp.array([0, 0, 1, 1], jnp.int32)[None]
    flip_y = jnp.where(c == 0, flip_a, flip_b)
    flip_x = jnp.where(c == 0, flip_b, flip_a)
    source = grid.join((z - steps) % line, y ^ flip_y, x ^ flip_x, c)
    gate_slot = table[source]
    gate_slot = jnp.where(c == 0, gate_slot, gate_slot[:, :, ::-1])
    taken = gate_slot > 0.0
    before = jnp.triu(jnp.ones((token_count, token_count), BF16), 1)
    ahead = jnp.dot(taken.astype(BF16), before, preferred_element_type=F32).astype(jnp.int32)
    slot = jnp.where(taken, ahead, room)
    picked = slot[:, :, :, None, :] == jnp.arange(room, dtype=jnp.int32)[:, None]
    select = picked.astype(BF16).transpose(0, 2, 1, 3, 4)
    row_gate = jnp.sum(jnp.where(picked, gate_slot[:, :, :, None, :], 0.0), axis=4).transpose(
        0, 2, 1, 3
    )

    other = grid.cross_core(weights)
    pair = (weights, other)
    current = jnp.concatenate([tokens, cotangent], axis=0)
    parts, kept, dots = [], [], []
    for r in range(line):
        near_a = grid.cross_a(current)
        near_b = grid.cross_b(current)
        far = grid.cross_b(near_a)
        part, keep, dot = chunk_compute(
            [current, near_a, near_b, far], select[r], row_gate[r], pair, width
        )
        parts.append(part)
        kept.append(keep)
        dots.append(dot)
        if r + 1 < line:
            current = grid.up(current)

    carried = None
    for r in reversed(range(line)):
        own, near_a, near_b, far = parts[r]
        passed = grid.cross_b(far)
        from_b = grid.cross_b(near_b)
        from_a = grid.cross_a(add(near_a, passed).astype(BF16))
        terms = [own, from_b, from_a] + ([carried] if carried is not None else [])
        total = add(*terms)
        if r:
            carried = grid.down(total.astype(BF16))
    result = total.astype(BF16)
    mixed, input_grad = result[:token_count], result[token_count:]

    dot_slot = jnp.stack(dots)
    dot_token = jnp.sum(
        select.astype(F32) * dot_slot[..., None], axis=3
    )
    dz, dy, dx_, _ = grid.split(expert_range)
    turn_y, turn_x = dy ^ y, dx_ ^ x
    kind_a = jnp.where(c == 0, turn_y, turn_x)
    kind_b = jnp.where(c == 0, turn_x, turn_y)
    back = dot_token.transpose(0, 2, 1, 3).reshape(line * 4, 2, token_count)[
        ((z - dz) % line) * 4 + kind_a + 2 * kind_b
    ]
    returned = lax.all_to_all(
        back.reshape(experts, 2 * token_count), BOTH, split_axis=0, concat_axis=0, tiled=True
    ).reshape(experts // 2, 2, 2, token_count)
    lane = jnp.where(c == 0, returned[:, 0], returned[:, 1, ::-1]).reshape(experts, token_count)
    gate_grad = jnp.sum(jnp.where(hit, lane.T[:, None, :], 0.0), axis=2)

    grad = []
    for e in range(2):
        row_e, cot_e, both, hidden = (
            jnp.concatenate([kept[r][e][i] for r in range(line)]) for i in range(4)
        )
        tn = (((0,), (0,)), ((), ()))
        grad.append(
            jnp.concatenate(
                [
                    lax.dot_general(row_e, both, tn, preferred_element_type=F32),
                    lax.dot_general(cot_e, hidden, tn, preferred_element_type=F32),
                ],
                axis=1,
            )
        )
    gradient = grad[0] + grid.cross_core(grad[1].astype(BF16)).astype(F32)
    clip_bound = clip_norm * experts ** (-0.5)
    scale = jnp.minimum(1.0, clip_bound / (jnp.sqrt(jnp.sum(gradient * gradient)) + 1e-06))
    scaled = scale * gradient
    first = beta_first * moment_first[0].astype(F32) + (1.0 - beta_first) * scaled
    second = beta_second * moment_second[0].astype(F32) + (1.0 - beta_second) * scaled * scaled
    update = first / bias_first / (jnp.sqrt(second / bias_second) + adam_eps)
    new_weights = (weights.astype(F32) - rate * update).astype(BF16)

    hot = hot_slot[0]
    new_other = grid.cross_core(new_weights)
    candidate = jnp.where(hot % 2 == c, new_weights, new_other)
    half = candidate.shape[0] // 2
    piece = grid.cross_side(lax.dynamic_slice_in_dim(candidate, c * half, half, 0))
    piece_other = grid.cross_core(piece)
    across = jnp.where(
        c == 0,
        jnp.concatenate([piece, piece_other]),
        jnp.concatenate([piece_other, piece]),
    )
    hot_copy = jnp.where(hot // 2 == x, candidate, across)
    return (mixed, input_grad, gate_grad, new_weights[None], hot_copy[None])


def solution(mesh):
    return jax.shard_map(
        shards,
        mesh=mesh,
        in_specs=(
            P(BOTH, None),
            P(BOTH, None),
            P(BOTH, None),
            P(BOTH, None),
            P(BOTH, None, None),
            P(BOTH, None, None),
            P(BOTH, None, None),
            P("expert"),
        ),
        out_specs=(
            P(BOTH, None),
            P(BOTH, None),
            P(BOTH, None),
            P(BOTH, None, None),
            P(BOTH, None, None),
        ),
        check_vma=False,
    )
```

```python
import jax
import jax.numpy as jnp
from jax import lax
from jax.experimental import pallas as pl
from jax.experimental.pallas import tpu as pltpu
from jax.sharding import PartitionSpec as P

beta_first = 0.9
beta_second = 0.95
adam_eps = 1e-08
rate = 0.05
clip_norm = 1.0
bias_first = 1.0 - 0.9**10
bias_second = 1.0 - 0.95**10
BOTH = ("expert", "replica")
F32 = jnp.float32
BF16 = jnp.bfloat16
EXTRA = 8
BRIEF = pl.CostEstimate(flops=1, transcendentals=0, bytes_accessed=1)


class Grid:
    def __init__(self, groups, owners):
        self.line = groups // 2
        self.sides = owners // 2
        self.owners = owners
        self.count = groups * owners

    def split(self, device):
        place, owner = device // self.owners, device % self.owners
        return place // 2, place % 2, owner // 2, owner % 2

    def join(self, line, row, side, core):
        return ((line * 2 + row) * self.sides + side) * 2 + core

    def move(self, value, step):
        pairs = [(d, self.join(*step(*self.split(d)))) for d in range(self.count)]
        return lax.ppermute(value, BOTH, pairs)

    def up(self, value):
        return self.move(value, lambda z, y, x, c: ((z + 1) % self.line, y, x, c))

    def down(self, value):
        return self.move(value, lambda z, y, x, c: ((z - 1) % self.line, y, x, c))

    def cross_a(self, value):
        return self.move(value, lambda z, y, x, c: (z, y ^ (1 - c), x ^ c, c))

    def cross_b(self, value):
        return self.move(value, lambda z, y, x, c: (z, y ^ c, x ^ (1 - c), c))

    def cross_side(self, value):
        return self.move(value, lambda z, y, x, c: (z, y, x ^ 1, c))

    def cross_core(self, value):
        return self.move(value, lambda z, y, x, c: (z, y, x, c ^ 1))


NT = (((1,), (1,)), ((), ()))
TN = (((0,), (0,)), ((), ()))


def dot(a, b, dims=(((1,), (0,)), ((), ()))):
    return lax.dot_general(a, b, dims, preferred_element_type=F32)


def chunk_body(step, room, token_count, width, *refs):
    spot, tok_near, tok_far, cot_near, cot_far, select, select_t, gate, w_own, w_other = refs[:10]
    refs = refs[10 + (4 if step else 0) :]
    near_out, far_out = refs[:2]
    kept_out = refs[2:6]
    w, rows, cots, both, hidden, y, dx, dots, sem_w, sem_k = refs[6:]
    loads = [pltpu.make_async_copy(ref, w.at[e], sem_w.at[e]) for e, ref in enumerate((w_own, w_other))]
    for load in loads:
        load.start()
    near_far = ((tok_near, tok_far, rows), (cot_near, cot_far, cots))
    for near, far, out in near_far:
        for q in range(4):
            block = (near, near, far, far)[q][(q % 2) * token_count : (q % 2 + 1) * token_count, :]
            taken = dot(select[q], block).astype(BF16)
            for e in range(2):
                out[e, q * room : (q + 1) * room, :] = taken[e * room : (e + 1) * room]
    saves = []
    for e in range(2):
        loads[e].wait()
        gate_up = dot(rows[e], w[e, :, : 2 * width])
        spread = dot(cots[e], w[e, :, 2 * width :])
        gate_in, up_in = gate_up[:, :width], gate_up[:, width:]
        sig = jax.nn.sigmoid(gate_in)
        active = gate_in * sig
        hid = active * up_in
        products = jnp.sum(hid * spread, axis=1, keepdims=True)
        row_gates = []
        for q in range(4):
            chosen = select[q, e * room : (e + 1) * room, :].astype(F32)
            row_gates.append(jnp.sum(chosen * gate[q, e : e + 1, :], axis=1, keepdims=True))
            dots[q, e : e + 1, :] = jnp.sum(
                chosen * products[q * room : (q + 1) * room], axis=0, keepdims=True
            )
        row_gate = jnp.concatenate(row_gates, axis=0)
        hidden[e] = (hid * row_gate).astype(BF16)
        grad = spread * row_gate
        both[e, :, :width] = (grad * up_in * sig * (1.0 + gate_in * (1.0 - sig))).astype(BF16)
        both[e, :, width:] = (grad * active).astype(BF16)
        for i, (src, out) in enumerate(zip((rows, cots, both, hidden), kept_out)):
            save = pltpu.make_async_copy(src.at[e], out.at[step, e], sem_k.at[i, e])
            save.start()
            saves.append(save)
        out_y = dot(hidden[e], w[e, :, 2 * width :], NT).astype(BF16)
        out_dx = dot(both[e], w[e, :, : 2 * width], NT).astype(BF16)
        for q in range(4):
            y[q, e * room : (e + 1) * room, :] = out_y[q * room : (q + 1) * room]
            dx[q, e * room : (e + 1) * room, :] = out_dx[q * room : (q + 1) * room]
    model = near_out.shape[1]
    for q in range(4):
        out = (near_out, near_out, far_out, far_out)[q]
        lines = token_count + EXTRA
        start = (q % 2) * lines
        out[start : start + token_count, :] = dot(select_t[q], y[q]).astype(BF16)
        pair = [dots[q, e : e + 1, :] for e in range(2)]
        even = jnp.where(spot[2] == 0, pair[0], pair[1])
        odd = jnp.where(spot[2] == 0, pair[1], pair[0])
        tiled = jnp.concatenate([even, odd] * (model // (2 * token_count)), axis=1)
        at_row = lax.broadcasted_iota(jnp.int32, (EXTRA, model), 0) == spot[0]
        at_lane = lax.broadcasted_iota(jnp.int32, (EXTRA, model), 1) // (2 * token_count) == spot[1]
        out[start + token_count : start + lines, :] = jnp.where(at_row & at_lane, tiled, 0.0).astype(BF16)
        start = 2 * lines + (q % 2) * token_count
        out[start : start + token_count, :] = dot(select_t[q], dx[q]).astype(BF16)
    for save in saves:
        save.wait()


def chunk(step, line, spot, blocks, select, select_t, gate, weights, kept, width):
    model = weights[0].shape[0]
    room, token_count = select.shape[1] // 2, select.shape[2]
    rows = 4 * room
    vmem = pl.BlockSpec(memory_space=pltpu.VMEM)
    hbm = pl.BlockSpec(memory_space=pl.ANY)
    block = jax.ShapeDtypeStruct((4 * token_count + 2 * EXTRA, model), BF16)
    sizes = (model, model, 2 * width, width)
    outs = (
        [block] * 2
        + [jax.ShapeDtypeStruct((line, 2, rows, n), BF16) for n in sizes]
    )

    def body(*refs):
        chunk_body(step, room, token_count, width, *refs)

    result = pl.pallas_call(
        body,
        out_shape=outs,
        in_specs=[pl.BlockSpec(memory_space=pltpu.SMEM)]
        + [vmem] * 7
        + [hbm] * (2 + (4 if step else 0)),
        out_specs=[vmem] * 2 + [hbm] * 4,
        scratch_shapes=[pltpu.VMEM((2, model, 3 * width), BF16)]
        + [pltpu.VMEM((2, rows, n), BF16) for n in sizes]
        + [pltpu.VMEM((4, 2 * room, model), BF16)] * 2
        + [pltpu.VMEM((4, 2, token_count), F32)]
        + [pltpu.SemaphoreType.DMA((2,)), pltpu.SemaphoreType.DMA((4, 2))],
        input_output_aliases={10 + i: 2 + i for i in range(4)} if step else {},
        compiler_params=pltpu.CompilerParams(vmem_limit_bytes=56 * 1024 * 1024),
        cost_estimate=BRIEF,
        name="chunk",
    )(spot, *blocks, select, select_t, gate, *weights, *(kept if step else []))
    return result[:2], result[2:]


def weight_grad(kept, expert, block_rows=256):
    rows, cots, both, hidden = kept
    line, _, count, model = rows.shape
    width = hidden.shape[3]

    def body(rows, cots, both, hidden, out):
        flat = [ref[...].reshape(line * count, ref.shape[3]) for ref in (rows, cots, both, hidden)]
        out[:, : 2 * width] = dot(flat[0], flat[2], TN).astype(BF16)
        out[:, 2 * width :] = dot(flat[1], flat[3], TN).astype(BF16)

    part = pl.BlockSpec((line, 1, count, block_rows), lambda i: (0, expert, 0, i))

    def whole(n):
        return pl.BlockSpec((line, 1, count, n), lambda i: (0, expert, 0, 0))

    return pl.pallas_call(
        body,
        grid=(model // block_rows,),
        out_shape=jax.ShapeDtypeStruct((model, 3 * width), BF16),
        in_specs=[part, part, whole(2 * width), whole(width)],
        out_specs=pl.BlockSpec((block_rows, 3 * width), lambda i: (i, 0)),
        compiler_params=pltpu.CompilerParams(vmem_limit_bytes=56 * 1024 * 1024),
        cost_estimate=BRIEF,
        name="weight_grad",
    )(rows, cots, both, hidden)


def clip_factor(mine, received, clip_bound, block_rows=256):
    model, columns = mine.shape
    count = model // block_rows

    def body(mine, received, out, squares):
        step = pl.program_id(0)

        @pl.when(step == 0)
        def _():
            squares[...] = jnp.zeros_like(squares)

        def add_rows(i, total):
            at = pl.ds(pl.multiple_of(i * 16, 16), 16)
            g = mine[at, :].astype(F32) + received[at, :].astype(F32)
            return total + jnp.sum((g * g).reshape(2, 8, columns), axis=0)

        squares[...] = lax.fori_loop(0, block_rows // 16, add_rows, squares[...], unroll=2)

        @pl.when(step == count - 1)
        def _():
            norm = jnp.sqrt(jnp.sum(squares[...], axis=(0, 1), keepdims=True))
            out[...] = jnp.broadcast_to(jnp.minimum(1.0, clip_bound / (norm + 1e-06)), out.shape)

    block = pl.BlockSpec((block_rows, columns), lambda i: (i, 0))
    return pl.pallas_call(
        body,
        grid=(count,),
        out_shape=jax.ShapeDtypeStruct((8, 128), F32),
        in_specs=[block, block],
        out_specs=pl.BlockSpec((8, 128), lambda i: (0, 0)),
        scratch_shapes=[pltpu.VMEM((8, columns), F32)],
        cost_estimate=BRIEF,
        name="clip_factor",
    )(mine, received)


def adam(half, factor, mine, received, weights, moment_first, moment_second, full, block_rows=256):
    model, columns = weights.shape
    count = model // 2 // block_rows

    def body(factor, mine, received, w, m, v, *refs):
        full, piece = refs[-2:]
        scale = factor[0:1, 0:1]

        def update_rows(i, carry):
            at = pl.ds(pl.multiple_of(i * 16, 16), 16)
            scaled = scale * (mine[at, :].astype(F32) + received[at, :].astype(F32))
            first = beta_first * m[at, :].astype(F32) + (1.0 - beta_first) * scaled
            second = beta_second * v[at, :].astype(F32) + (1.0 - beta_second) * scaled * scaled
            root = jnp.sqrt(second * (1.0 / bias_second)) + adam_eps
            value = (w[at, :].astype(F32) - (rate / bias_first) * first / root).astype(BF16)
            full[at, :] = value
            piece[at, :] = value
            return carry

        lax.fori_loop(0, block_rows // 16, update_rows, 0)

    block = pl.BlockSpec((block_rows, columns), lambda i: (half * count + i, 0))
    given = [] if full is None else [full]
    return pl.pallas_call(
        body,
        grid=(count,),
        out_shape=[
            jax.ShapeDtypeStruct((model, columns), BF16),
            jax.ShapeDtypeStruct((model // 2, columns), BF16),
        ],
        in_specs=[pl.BlockSpec((8, 128), lambda i: (0, 0))]
        + [block] * 5
        + [pl.BlockSpec(memory_space=pl.ANY)] * len(given),
        out_specs=[block, pl.BlockSpec((block_rows, columns), lambda i: (i, 0))],
        input_output_aliases={6: 0} if given else {},
        cost_estimate=BRIEF,
        name="adam",
    )(factor, mine, received, weights, moment_first, moment_second, *given)


def place_hot(half, flags, own, other, direct, relayed, full):
    rows, columns = own.shape
    block_rows = rows // 4
    spot = jax.ShapeDtypeStruct((2 * rows, columns), BF16)

    def body(flags, own, other, direct, relayed, *refs):
        here, mine = flags[0] == 1, flags[1] == 1
        first = (pl.program_id(0) < 2) == (flags[2] == 0)
        for wanted, ref in (
            (here & mine, own),
            (here & ~mine, other),
            (~here & first, direct),
            (~here & ~first, relayed),
        ):

            @pl.when(wanted)
            def _(ref=ref):
                refs[-1][...] = ref[...]

    def spec(where):
        return pl.BlockSpec((block_rows, columns), lambda i, flags: (where(i, flags), 0))

    given = [] if full is None else [full]
    return pl.pallas_call(
        body,
        out_shape=spot,
        grid_spec=pltpu.PrefetchScalarGridSpec(
            num_scalar_prefetch=1,
            grid=(4,),
            in_specs=[
                spec(lambda i, f: i * f[0] * f[1]),
                spec(lambda i, f: i * f[0] * (1 - f[1])),
                spec(lambda i, f: (1 - f[0]) * jnp.clip(i - 2 * f[2], 0, 1)),
                spec(lambda i, f: (1 - f[0]) * jnp.clip(i - 2 * (1 - f[2]), 0, 1)),
            ]
            + [pl.BlockSpec(memory_space=pl.ANY)] * len(given),
            out_specs=spec(lambda i, f: 4 * half + i),
        ),
        input_output_aliases={5: 0} if given else {},
        cost_estimate=BRIEF,
        name="place_hot",
    )(flags, own, other, direct, relayed, *given)


def combine(near, back, before, last):
    rows, columns = near.shape
    n = (rows - 2 * EXTRA) // 4
    m = n + EXTRA
    width = columns // 4
    up_rows = m if last else (2 * n if before is None else 2 * n + m)
    sizes = [m, m + n if last else m, up_rows] + ([n] if last else [])

    def body(*refs):
        given, outs = refs[: -len(sizes)], refs[-len(sizes) :]
        own, across, up = outs[:3]
        near, back = given[:2]

        def part(start, count):
            at = slice(start, start + count)
            return near[at, :].astype(F32) + back[at, :].astype(F32)

        own[...] = part(0, m).astype(BF16)
        across[:m, :] = part(m, m).astype(BF16)
        grads = part(2 * m, 2 * n)
        if before is not None:
            old_own, old_across, old_up = given[2:]
            grads = grads + old_up[: 2 * n, :].astype(F32)
            waiting = old_own[...].astype(F32) + old_across[...].astype(F32)
            if before[2].shape[0] > 2 * n:
                waiting = waiting + old_up[2 * n :, :].astype(F32)
            up[up_rows - m :, :] = waiting.astype(BF16)
        if last:
            outs[3][...] = grads[:n].astype(BF16)
            across[m:, :] = grads[n:].astype(BF16)
        else:
            up[: 2 * n, :] = grads.astype(BF16)

    given = [near, back] + ([] if before is None else list(before))
    return pl.pallas_call(
        body,
        grid=(4,),
        out_shape=[jax.ShapeDtypeStruct((size, columns), BF16) for size in sizes],
        in_specs=[pl.BlockSpec((v.shape[0], width), lambda i: (0, i)) for v in given],
        out_specs=[pl.BlockSpec((size, width), lambda i: (0, i)) for size in sizes],
        cost_estimate=BRIEF,
        name="combine",
    )(*given)


def stage(*values):
    return lax.optimization_barrier(values)


def add(*values):
    total = values[0].astype(F32)
    for value in values[1:]:
        total = total + value.astype(F32)
    return total


def shards(
    tokens, expert_ids, gates, cotangent, expert_weights, moment_first, moment_second, hot_slot
):
    groups = lax.axis_size("expert")
    owners = lax.axis_size("replica")
    experts = groups * owners
    grid = Grid(groups, owners)
    line = grid.line
    token_count, chosen = expert_ids.shape
    width = expert_weights.shape[2] // 3
    room = 2 * token_count * chosen // experts
    device = lax.axis_index("expert") * owners + lax.axis_index("replica")
    z, y, x, c = grid.split(device)
    weights = expert_weights[0]

    expert_range = jnp.arange(experts, dtype=jnp.int32)
    hit = expert_ids[:, :, None] == expert_range
    gate_table = jnp.sum(jnp.where(hit, gates[:, :, None], 0.0), axis=1).T
    by_chip = gate_table.reshape(experts // 2, 1, 2, token_count)
    send = jnp.broadcast_to(by_chip, (experts // 2, 2, 2, token_count))
    table = lax.all_to_all(
        send.reshape(experts, 2 * token_count), BOTH, split_axis=0, concat_axis=0, tiled=True
    ).reshape(experts, 2, token_count)
    def route(table):
        steps = jnp.arange(line, dtype=jnp.int32)[:, None]
        flip_a = jnp.array([0, 1, 0, 1], jnp.int32)[None]
        flip_b = jnp.array([0, 0, 1, 1], jnp.int32)[None]
        flip_y = jnp.where(c == 0, flip_a, flip_b)
        flip_x = jnp.where(c == 0, flip_b, flip_a)
        source = grid.join((z - steps) % line, y ^ flip_y, x ^ flip_x, c)
        gate_slot = table[source]
        gate_slot = jnp.where(c == 0, gate_slot, gate_slot[:, :, ::-1])
        taken = gate_slot > 0.0
        before = jnp.triu(jnp.ones((token_count, token_count), BF16), 1)
        ahead = jnp.dot(taken.astype(BF16), before, preferred_element_type=F32).astype(jnp.int32)
        slot = jnp.where(taken, ahead, room)
        places = jnp.arange(room, dtype=jnp.int32)
        select = (slot[:, :, :, None, :] == places[:, None]).astype(BF16)
        select = select.reshape(line, 4, 2 * room, token_count)
        select_t = (slot.transpose(0, 1, 3, 2)[..., None] == places).astype(BF16)
        select_t = select_t.reshape(line, 4, token_count, 2 * room)
        return select, select_t, gate_slot

    per_row = expert_weights.shape[1] // (2 * token_count)
    chip = device // 2
    spot = jnp.stack([chip // per_row, chip % per_row, c]).astype(jnp.int32)

    def run_chunk(r, kept):
        return chunk(r, line, spot, blocks[r], select[r], select_t[r], gate_slot[r], pair, kept, width)

    tok, tok_a, cot_near, pair = stage(
        (tokens, grid.up(tokens)),
        grid.cross_a(tokens),
        jnp.concatenate([cotangent, grid.cross_a(cotangent)]),
        (weights, grid.cross_core(weights)),
    )
    tok = list(tok)
    blocks, parts, kept = [], [], []
    tok_near = jnp.concatenate([tok[0], tok_a])
    for r in range(line):
        far = (grid.cross_b(tok_near), grid.cross_b(cot_near))
        more = {}
        if r + 1 < line:
            more["cot"] = grid.up(cot_near)
            more["a"] = grid.cross_a(tok[r + 1])
        if r + 2 < line:
            more["tok"] = grid.up(tok[r + 1])
        done = None
        if r:
            done = run_chunk(r - 1, kept)
        ready = (tok_near, far[0], cot_near, far[1])
        if r == 0:
            ready, more, table = stage(ready, more, table)
            select, select_t, gate_slot = route(table)
        else:
            ready, more, done, parts = stage(ready, more, done, parts)
        blocks.append(list(ready))
        if done is not None:
            part, kept = done
            parts.append(part)
        if r + 1 < line:
            cot_near = more["cot"]
            tok_near = jnp.concatenate([tok[r + 1], more["a"]])
        if r + 2 < line:
            tok.append(more["tok"])

    order = list(range(1, line)) + [0]
    back = grid.cross_b(parts[order[0]][1])
    part, kept = run_chunk(line - 1, kept)
    back, part, kept, other_grad = stage(back, part, kept, weight_grad(kept, 1))
    back = {order[0]: back}
    parts.append(part)

    before = None
    for i, r in enumerate(order):
        last = i + 1 == line
        own, across, up, *dx_own = combine(parts[r][0], back[r], before, last)
        moves = [grid.cross_a(across), grid.up(up)]
        coming = order[i + 1 : i + 2] if i != 1 else order[2:3] + order[-1:]
        coming = [n for n in coming if n not in back]
        more = [grid.cross_b(parts[n][1]) for n in coming]
        work = ()
        if i == 0:
            work = (grid.cross_core(other_grad), weight_grad(kept, 0))
        if i == 1:
            factor = clip_factor(mine, received, clip_norm * experts ** (-0.5))
            given = (factor, mine, received, weights, moment_first[0], moment_second[0])
            full, new_0 = adam(0, *given, None)
            full, new_1 = adam(1, *given, full)
            work = (full, new_0, new_1)
        moves, more, work, own, dx_own = stage(moves, more, work, own, dx_own)
        if i == 0:
            received, mine = work
        if i == 1:
            full, new_0, new_1 = work
        back.update(zip(coming, more))
        before = (own, *moves)
    total = add(own, moves[0][: token_count + EXTRA], moves[1])
    mixed = total[:token_count].astype(BF16)
    input_grad = add(dx_own[0], moves[0][token_count + EXTRA :]).astype(BF16)
    by_expert = total[token_count:].reshape(-1)[: experts * token_count]
    by_expert = by_expert.reshape(experts, token_count)
    gate_grad = jnp.sum(jnp.where(hit, by_expert.T[:, None, :], 0.0), axis=2)

    hot = hot_slot[0]
    is_mine = hot % 2 == c
    flags = jnp.stack([hot // 2 == x, is_mine, c == 1]).astype(jnp.int32)
    def pick(piece, other):
        size = piece.shape[0] // 2
        part_own = lax.dynamic_slice_in_dim(piece, c * size, size, 0)
        part_other = lax.dynamic_slice_in_dim(other, c * size, size, 0)
        return jnp.where(is_mine, part_own, part_other)

    other_0, other_1 = grid.cross_core(new_0), grid.cross_core(new_1)
    direct_0, picked = stage(grid.cross_side(pick(new_0, other_0)), pick(new_1, other_1))
    direct_1 = grid.cross_side(picked)
    hot_copy = place_hot(0, flags, new_0, other_0, direct_0, grid.cross_core(direct_0), None)
    hot_copy, direct_1 = stage(hot_copy, direct_1)
    hot_copy = place_hot(1, flags, new_1, other_1, direct_1, grid.cross_core(direct_1), hot_copy)

    new_weights = full
    return (mixed, input_grad, gate_grad, new_weights[None], hot_copy[None])


def solution(mesh):
    return jax.shard_map(
        shards,
        mesh=mesh,
        in_specs=(
            P(BOTH, None),
            P(BOTH, None),
            P(BOTH, None),
            P(BOTH, None),
            P(BOTH, None, None),
            P(BOTH, None, None),
            P(BOTH, None, None),
            P("expert"),
        ),
        out_specs=(
            P(BOTH, None),
            P(BOTH, None),
            P(BOTH, None),
            P(BOTH, None, None),
            P(BOTH, None, None),
        ),
        check_vma=False,
    )
```

```python
import jax
import jax.numpy as jnp
from jax import lax
from jax.experimental import pallas as pl
from jax.experimental.pallas import tpu as pltpu
from jax.sharding import PartitionSpec as P

beta_first = 0.9
beta_second = 0.95
adam_eps = 1e-08
rate = 0.05
clip_norm = 1.0
bias_first = 1.0 - 0.9**10
bias_second = 1.0 - 0.95**10
BOTH = ("expert", "replica")
F32 = jnp.float32
BF16 = jnp.bfloat16
EXTRA = 8
BRIEF = pl.CostEstimate(flops=1, transcendentals=0, bytes_accessed=1)


class Grid:
    def __init__(self, groups, owners):
        self.line = groups // 2
        self.sides = owners // 2
        self.owners = owners
        self.count = groups * owners

    def split(self, device):
        place, owner = device // self.owners, device % self.owners
        return place // 2, place % 2, owner // 2, owner % 2

    def join(self, line, row, side, core):
        return ((line * 2 + row) * self.sides + side) * 2 + core

    def move(self, value, step):
        pairs = [(d, self.join(*step(*self.split(d)))) for d in range(self.count)]
        return lax.ppermute(value, BOTH, pairs)

    def up(self, value):
        return self.move(value, lambda z, y, x, c: ((z + 1) % self.line, y, x, c))

    def down(self, value):
        return self.move(value, lambda z, y, x, c: ((z - 1) % self.line, y, x, c))

    def cross_a(self, value):
        return self.move(value, lambda z, y, x, c: (z, y ^ (1 - c), x ^ c, c))

    def cross_b(self, value):
        return self.move(value, lambda z, y, x, c: (z, y ^ c, x ^ (1 - c), c))

    def cross_side(self, value):
        return self.move(value, lambda z, y, x, c: (z, y, x ^ 1, c))

    def cross_core(self, value):
        return self.move(value, lambda z, y, x, c: (z, y, x, c ^ 1))


NT = (((1,), (1,)), ((), ()))
TN = (((0,), (0,)), ((), ()))


def dot(a, b, dims=(((1,), (0,)), ((), ()))):
    return lax.dot_general(a, b, dims, preferred_element_type=F32)


def chunk_body(step, room, token_count, width, *refs):
    spot, tok_near, tok_far, cot_near, cot_far, select, select_t, gate, w_own, w_other = refs[:10]
    refs = refs[10 + (4 if step else 0) :]
    near_out, far_out = refs[:2]
    kept_out = refs[2:6]
    w, rows, cots, both, hidden, y, dx, dots, sem_w, sem_k = refs[6:]
    loads = [pltpu.make_async_copy(ref, w.at[e], sem_w.at[e]) for e, ref in enumerate((w_own, w_other))]
    for load in loads:
        load.start()
    near_far = ((tok_near, tok_far, rows), (cot_near, cot_far, cots))
    for near, far, out in near_far:
        for q in range(4):
            block = (near, near, far, far)[q][(q % 2) * token_count : (q % 2 + 1) * token_count, :]
            taken = dot(select[q], block).astype(BF16)
            for e in range(2):
                out[e, q * room : (q + 1) * room, :] = taken[e * room : (e + 1) * room]
    saves = []
    for e in range(2):
        loads[e].wait()
        gate_up = dot(rows[e], w[e, :, : 2 * width])
        spread = dot(cots[e], w[e, :, 2 * width :])
        gate_in, up_in = gate_up[:, :width], gate_up[:, width:]
        sig = jax.nn.sigmoid(gate_in)
        active = gate_in * sig
        hid = active * up_in
        products = jnp.sum(hid * spread, axis=1, keepdims=True)
        row_gates = []
        for q in range(4):
            chosen = select[q, e * room : (e + 1) * room, :].astype(F32)
            row_gates.append(jnp.sum(chosen * gate[q, e : e + 1, :], axis=1, keepdims=True))
            dots[q, e : e + 1, :] = jnp.sum(
                chosen * products[q * room : (q + 1) * room], axis=0, keepdims=True
            )
        row_gate = jnp.concatenate(row_gates, axis=0)
        hidden[e] = (hid * row_gate).astype(BF16)
        grad = spread * row_gate
        both[e, :, :width] = (grad * up_in * sig * (1.0 + gate_in * (1.0 - sig))).astype(BF16)
        both[e, :, width:] = (grad * active).astype(BF16)
        for i, (src, out) in enumerate(zip((rows, cots, both, hidden), kept_out)):
            save = pltpu.make_async_copy(src.at[e], out.at[step, e], sem_k.at[i, e])
            save.start()
            saves.append(save)
        out_y = dot(hidden[e], w[e, :, 2 * width :], NT).astype(BF16)
        out_dx = dot(both[e], w[e, :, : 2 * width], NT).astype(BF16)
        for q in range(4):
            y[q, e * room : (e + 1) * room, :] = out_y[q * room : (q + 1) * room]
            dx[q, e * room : (e + 1) * room, :] = out_dx[q * room : (q + 1) * room]
    model = near_out.shape[1]
    full_at = pl.multiple_of(spot[3] * room, room)
    rest_at = pl.multiple_of((1 - spot[3]) * room, room)
    for q in range(4):
        far = q > 1
        out = far_out if far else near_out
        size = room + room // 2 if far else token_count
        lines = size + EXTRA
        for src, start in ((y, (q % 2) * lines), (dx, 2 * lines + (q % 2) * size)):
            if far:
                out[start : start + room, :] = src[q, pl.ds(full_at, room), :]
                out[start + room : start + size, :] = src[q, pl.ds(rest_at, room // 2), :]
            else:
                out[start : start + size, :] = dot(select_t[q], src[q]).astype(BF16)
        pair = [dots[q, e : e + 1, :] for e in range(2)]
        even = jnp.where(spot[2] == 0, pair[0], pair[1])
        odd = jnp.where(spot[2] == 0, pair[1], pair[0])
        tiled = jnp.concatenate([even, odd] * (model // (2 * token_count)), axis=1)
        at_row = lax.broadcasted_iota(jnp.int32, (EXTRA, model), 0) == spot[0]
        at_lane = lax.broadcasted_iota(jnp.int32, (EXTRA, model), 1) // (2 * token_count) == spot[1]
        start = (q % 2) * lines + size
        out[start : start + EXTRA, :] = jnp.where(at_row & at_lane, tiled, 0.0).astype(BF16)
    for save in saves:
        save.wait()


def chunk(step, line, spot, blocks, select, select_t, gate, weights, kept, width):
    model = weights[0].shape[0]
    room, token_count = select.shape[1] // 2, select.shape[2]
    rows = 4 * room
    vmem = pl.BlockSpec(memory_space=pltpu.VMEM)
    hbm = pl.BlockSpec(memory_space=pl.ANY)
    near = jax.ShapeDtypeStruct((4 * token_count + 2 * EXTRA, model), BF16)
    far = jax.ShapeDtypeStruct((6 * room + 2 * EXTRA, model), BF16)
    sizes = (model, model, 2 * width, width)
    outs = (
        [near, far]
        + [jax.ShapeDtypeStruct((line, 2, rows, n), BF16) for n in sizes]
    )

    def body(*refs):
        chunk_body(step, room, token_count, width, *refs)

    result = pl.pallas_call(
        body,
        out_shape=outs,
        in_specs=[pl.BlockSpec(memory_space=pltpu.SMEM)]
        + [vmem] * 7
        + [hbm] * (2 + (4 if step else 0)),
        out_specs=[vmem] * 2 + [hbm] * 4,
        scratch_shapes=[pltpu.VMEM((2, model, 3 * width), BF16)]
        + [pltpu.VMEM((2, rows, n), BF16) for n in sizes]
        + [pltpu.VMEM((4, 2 * room, model), BF16)] * 2
        + [pltpu.VMEM((4, 2, token_count), F32)]
        + [pltpu.SemaphoreType.DMA((2,)), pltpu.SemaphoreType.DMA((4, 2))],
        input_output_aliases={10 + i: 2 + i for i in range(4)} if step else {},
        compiler_params=pltpu.CompilerParams(vmem_limit_bytes=56 * 1024 * 1024),
        cost_estimate=BRIEF,
        name="chunk",
    )(spot, *blocks, select, select_t, gate, *weights, *(kept if step else []))
    return result[:2], result[2:]


def weight_grad(kept, expert, block_rows=256):
    rows, cots, both, hidden = kept
    line, _, count, model = rows.shape
    width = hidden.shape[3]

    def body(rows, cots, both, hidden, out):
        flat = [ref[...].reshape(line * count, ref.shape[3]) for ref in (rows, cots, both, hidden)]
        out[:, : 2 * width] = dot(flat[0], flat[2], TN).astype(BF16)
        out[:, 2 * width :] = dot(flat[1], flat[3], TN).astype(BF16)

    part = pl.BlockSpec((line, 1, count, block_rows), lambda i: (0, expert, 0, i))

    def whole(n):
        return pl.BlockSpec((line, 1, count, n), lambda i: (0, expert, 0, 0))

    return pl.pallas_call(
        body,
        grid=(model // block_rows,),
        out_shape=jax.ShapeDtypeStruct((model, 3 * width), BF16),
        in_specs=[part, part, whole(2 * width), whole(width)],
        out_specs=pl.BlockSpec((block_rows, 3 * width), lambda i: (i, 0)),
        compiler_params=pltpu.CompilerParams(vmem_limit_bytes=56 * 1024 * 1024),
        cost_estimate=BRIEF,
        name="weight_grad",
    )(rows, cots, both, hidden)


def clip_factor(mine, received, clip_bound, block_rows=256):
    model, columns = mine.shape
    count = model // block_rows

    def body(mine, received, out, squares):
        step = pl.program_id(0)

        @pl.when(step == 0)
        def _():
            squares[...] = jnp.zeros_like(squares)

        def add_rows(i, total):
            at = pl.ds(pl.multiple_of(i * 16, 16), 16)
            g = mine[at, :].astype(F32) + received[at, :].astype(F32)
            return total + jnp.sum((g * g).reshape(2, 8, columns), axis=0)

        squares[...] = lax.fori_loop(0, block_rows // 16, add_rows, squares[...], unroll=2)

        @pl.when(step == count - 1)
        def _():
            norm = jnp.sqrt(jnp.sum(squares[...], axis=(0, 1), keepdims=True))
            out[...] = jnp.broadcast_to(jnp.minimum(1.0, clip_bound / (norm + 1e-06)), out.shape)

    block = pl.BlockSpec((block_rows, columns), lambda i: (i, 0))
    return pl.pallas_call(
        body,
        grid=(count,),
        out_shape=jax.ShapeDtypeStruct((8, 128), F32),
        in_specs=[block, block],
        out_specs=pl.BlockSpec((8, 128), lambda i: (0, 0)),
        scratch_shapes=[pltpu.VMEM((8, columns), F32)],
        cost_estimate=BRIEF,
        name="clip_factor",
    )(mine, received)


def adam(half, factor, mine, received, weights, moment_first, moment_second, full, block_rows=256):
    model, columns = weights.shape
    count = model // 2 // block_rows

    def body(factor, mine, received, w, m, v, *refs):
        full, piece = refs[-2:]
        scale = factor[0:1, 0:1]

        def update_rows(i, carry):
            at = pl.ds(pl.multiple_of(i * 16, 16), 16)
            scaled = scale * (mine[at, :].astype(F32) + received[at, :].astype(F32))
            first = beta_first * m[at, :].astype(F32) + (1.0 - beta_first) * scaled
            second = beta_second * v[at, :].astype(F32) + (1.0 - beta_second) * scaled * scaled
            root = jnp.sqrt(second * (1.0 / bias_second)) + adam_eps
            value = (w[at, :].astype(F32) - (rate / bias_first) * first / root).astype(BF16)
            full[at, :] = value
            piece[at, :] = value
            return carry

        lax.fori_loop(0, block_rows // 16, update_rows, 0)

    block = pl.BlockSpec((block_rows, columns), lambda i: (half * count + i, 0))
    given = [] if full is None else [full]
    return pl.pallas_call(
        body,
        grid=(count,),
        out_shape=[
            jax.ShapeDtypeStruct((model, columns), BF16),
            jax.ShapeDtypeStruct((model // 2, columns), BF16),
        ],
        in_specs=[pl.BlockSpec((8, 128), lambda i: (0, 0))]
        + [block] * 5
        + [pl.BlockSpec(memory_space=pl.ANY)] * len(given),
        out_specs=[block, pl.BlockSpec((block_rows, columns), lambda i: (i, 0))],
        input_output_aliases={6: 0} if given else {},
        cost_estimate=BRIEF,
        name="adam",
    )(factor, mine, received, weights, moment_first, moment_second, *given)


def place_hot(half, flags, own, other, direct, relayed, full):
    rows, columns = own.shape
    block_rows = rows // 4
    spot = jax.ShapeDtypeStruct((2 * rows, columns), BF16)

    def body(flags, own, other, direct, relayed, *refs):
        here, mine = flags[0] == 1, flags[1] == 1
        first = (pl.program_id(0) < 2) == (flags[2] == 0)
        for wanted, ref in (
            (here & mine, own),
            (here & ~mine, other),
            (~here & first, direct),
            (~here & ~first, relayed),
        ):

            @pl.when(wanted)
            def _(ref=ref):
                refs[-1][...] = ref[...]

    def spec(where):
        return pl.BlockSpec((block_rows, columns), lambda i, flags: (where(i, flags), 0))

    given = [] if full is None else [full]
    return pl.pallas_call(
        body,
        out_shape=spot,
        grid_spec=pltpu.PrefetchScalarGridSpec(
            num_scalar_prefetch=1,
            grid=(4,),
            in_specs=[
                spec(lambda i, f: i * f[0] * f[1]),
                spec(lambda i, f: i * f[0] * (1 - f[1])),
                spec(lambda i, f: (1 - f[0]) * jnp.clip(i - 2 * f[2], 0, 1)),
                spec(lambda i, f: (1 - f[0]) * jnp.clip(i - 2 * (1 - f[2]), 0, 1)),
            ]
            + [pl.BlockSpec(memory_space=pl.ANY)] * len(given),
            out_specs=spec(lambda i, f: 4 * half + i),
        ),
        input_output_aliases={5: 0} if given else {},
        cost_estimate=BRIEF,
        name="place_hot",
    )(flags, own, other, direct, relayed, *given)


def combine(near, back, expand, before, last):
    rows, columns = near.shape
    n = (rows - 2 * EXTRA) // 4
    m, k = n + EXTRA, expand.shape[2]
    width = columns // 4
    up_rows = m if last else (2 * n if before is None else 2 * n + m)
    sizes = [m, m + n if last else m, up_rows] + ([n] if last else [])

    def body(*refs):
        given, outs = refs[: -len(sizes)], refs[-len(sizes) :]
        own, across, up = outs[:3]
        near, back, expand = given[:3]

        def plain(at, came):
            return near[at : at + EXTRA, :].astype(F32) + back[came : came + EXTRA, :].astype(F32)

        def part(i, at, came):
            return near[at : at + n, :].astype(F32) + dot(expand[i], back[came : came + k, :])

        for i, out in enumerate((own, across)):
            out[:n, :] = part(i, i * m, i * (k + EXTRA)).astype(BF16)
            out[n:m, :] = plain(i * m + n, i * (k + EXTRA) + k).astype(BF16)
        came = 2 * (k + EXTRA)
        grads = jnp.concatenate([part(i, 2 * m + i * n, came + i * k) for i in range(2)])
        if before is not None:
            old_own, old_across, old_up = given[3:]
            grads = grads + old_up[: 2 * n, :].astype(F32)
            waiting = old_own[...].astype(F32) + old_across[...].astype(F32)
            if before[2].shape[0] > 2 * n:
                waiting = waiting + old_up[2 * n :, :].astype(F32)
            up[up_rows - m :, :] = waiting.astype(BF16)
        if last:
            outs[3][...] = grads[:n].astype(BF16)
            across[m:, :] = grads[n:].astype(BF16)
        else:
            up[: 2 * n, :] = grads.astype(BF16)

    given = [near, back, expand] + ([] if before is None else list(before))
    return pl.pallas_call(
        body,
        grid=(4,),
        out_shape=[jax.ShapeDtypeStruct((size, columns), BF16) for size in sizes],
        in_specs=[
            pl.BlockSpec(v.shape, lambda i: (0, 0, 0))
            if v is expand
            else pl.BlockSpec((v.shape[0], width), lambda i: (0, i))
            for v in given
        ],
        out_specs=[pl.BlockSpec((size, width), lambda i: (0, i)) for size in sizes],
        cost_estimate=BRIEF,
        name="combine",
    )(*given)


def stage(*values):
    return lax.optimization_barrier(values)


def add(*values):
    total = values[0].astype(F32)
    for value in values[1:]:
        total = total + value.astype(F32)
    return total


def shards(
    tokens, expert_ids, gates, cotangent, expert_weights, moment_first, moment_second, hot_slot
):
    groups = lax.axis_size("expert")
    owners = lax.axis_size("replica")
    experts = groups * owners
    grid = Grid(groups, owners)
    line = grid.line
    token_count, chosen = expert_ids.shape
    width = expert_weights.shape[2] // 3
    room = 2 * token_count * chosen // experts
    device = lax.axis_index("expert") * owners + lax.axis_index("replica")
    z, y, x, c = grid.split(device)
    weights = expert_weights[0]

    expert_range = jnp.arange(experts, dtype=jnp.int32)
    hit = expert_ids[:, :, None] == expert_range
    gate_table = jnp.sum(jnp.where(hit, gates[:, :, None], 0.0), axis=1).T
    places = [grid.split(d) for d in range(experts)]
    met = [
        d // 2 * 2 + e for d in range(experts) for e in range(2)
    ], [
        grid.join(pz, py ^ pc, px ^ (1 - pc), 0) + e for pz, py, px, pc in places for e in range(2)
    ]
    wanted = jnp.array(met, jnp.int32).reshape(2, experts, 2).transpose(1, 0, 2).reshape(-1)
    table = lax.all_to_all(
        gate_table[wanted].reshape(experts, 4 * token_count),
        BOTH,
        split_axis=0,
        concat_axis=0,
        tiled=True,
    ).reshape(experts, 4, token_count)

    def route(table):
        steps = jnp.arange(line, dtype=jnp.int32)[:, None]
        flip_a = jnp.array([0, 1, 0, 1], jnp.int32)[None]
        flip_b = jnp.array([0, 0, 1, 1], jnp.int32)[None]
        flip_y = jnp.where(c == 0, flip_a, flip_b)
        flip_x = jnp.where(c == 0, flip_b, flip_a)
        source = grid.join((z - steps) % line, y ^ flip_y, x ^ flip_x, c)
        gate_slot = table[source][:, :, :2]
        gate_slot = jnp.where(c == 0, gate_slot, gate_slot[:, :, ::-1])
        taken = gate_slot > 0.0
        before = jnp.triu(jnp.ones((token_count, token_count), BF16), 1)
        ahead = jnp.dot(taken.astype(BF16), before, preferred_element_type=F32).astype(jnp.int32)
        slot = jnp.where(taken, ahead, room)
        places = jnp.arange(room, dtype=jnp.int32)
        select = (slot[:, :, :, None, :] == places[:, None]).astype(BF16)
        select = select.reshape(line, 4, 2 * room, token_count)
        select_t = (slot.transpose(0, 1, 3, 2)[..., None] == places).astype(BF16)
        select_t = select_t.reshape(line, 4, token_count, 2 * room)
        counts = jnp.sum((table[source[0, 0]] > 0.0).astype(jnp.int32), axis=1)
        fuller = (counts[1::2] > room // 2).astype(jnp.int32)
        there = table[source[:, :2]][:, :, 2:]
        there = jnp.where(fuller[1] == 1, there[:, :, ::-1], there) > 0.0
        spread = jnp.dot(there.astype(BF16), before, preferred_element_type=F32).astype(jnp.int32)
        spread = jnp.where(there, spread, room).transpose(0, 1, 3, 2)[..., None]
        expand = jnp.concatenate(
            [spread[:, :, :, 0] == places, spread[:, :, :, 1] == places[: room // 2]], axis=3
        ).astype(BF16)
        here = jnp.where(fuller[0] == c, 0, 1)
        return select, select_t, gate_slot, expand, here

    per_row = expert_weights.shape[1] // (2 * token_count)
    chip = device // 2

    def run_chunk(r, kept):
        return chunk(r, line, spot, blocks[r], select[r], select_t[r], gate_slot[r], pair, kept, width)

    pair = (weights, grid.cross_core(weights))
    tok = (tokens, grid.up(tokens))
    tok_a, cot_near = stage(
        grid.cross_a(tokens), jnp.concatenate([cotangent, grid.cross_a(cotangent)])
    )
    tok = list(tok)
    blocks, parts, kept = [], [], []
    tok_near = jnp.concatenate([tok[0], tok_a])
    for r in range(line):
        far = (grid.cross_b(tok_near), grid.cross_b(cot_near))
        more = {}
        if r + 1 < line:
            more["cot"] = grid.up(cot_near)
            more["a"] = grid.cross_a(tok[r + 1])
        if r + 2 < line:
            more["tok"] = grid.up(tok[r + 1])
        done = None
        if r:
            done = run_chunk(r - 1, kept)
        ready = (tok_near, far[0], cot_near, far[1])
        if r == 0:
            ready, more, table, pair, tok = stage(ready, more, table, pair, tok)
            select, select_t, gate_slot, expand, here = route(table)
            spot = jnp.stack([chip // per_row, chip % per_row, c, here]).astype(jnp.int32)
        else:
            ready, more, done, parts = stage(ready, more, done, parts)
        blocks.append(list(ready))
        if done is not None:
            part, kept = done
            parts.append(part)
        if r + 1 < line:
            cot_near = more["cot"]
            tok_near = jnp.concatenate([tok[r + 1], more["a"]])
        if r + 2 < line:
            tok.append(more["tok"])

    order = list(range(1, line)) + [0]
    back = grid.cross_b(parts[order[0]][1])
    part, kept = run_chunk(line - 1, kept)
    back, part, kept, other_grad, parts = stage(back, part, kept, weight_grad(kept, 1), parts)
    back = {order[0]: back}
    parts.append(part)

    before = None
    for i, r in enumerate(order):
        last = i + 1 == line
        own, across, up, *dx_own = combine(parts[r][0], back[r], expand[r], before, last)
        moves = [grid.cross_a(across), grid.up(up)]
        coming = order[i + 1 : i + 2] if i != 1 else order[2:3] + order[-1:]
        coming = [n for n in coming if n not in back]
        more = [grid.cross_b(parts[n][1]) for n in coming]
        work = ()
        if i == 0:
            work = (grid.cross_core(other_grad), weight_grad(kept, 0))
        if i == 1:
            factor = clip_factor(mine, received, clip_norm * experts ** (-0.5))
            given = (factor, mine, received, weights, moment_first[0], moment_second[0])
            full, new_0 = adam(0, *given, None)
            full, new_1 = adam(1, *given, full)
            work = (full, new_0, new_1)
        moves, more, work, own, dx_own, parts = stage(moves, more, work, own, dx_own, parts)
        if i == 0:
            received, mine = work
        if i == 1:
            full, new_0, new_1 = work
        back.update(zip(coming, more))
        before = (own, *moves)
    total = add(own, moves[0][: token_count + EXTRA], moves[1])
    mixed = total[:token_count].astype(BF16)
    input_grad = add(dx_own[0], moves[0][token_count + EXTRA :]).astype(BF16)
    by_expert = total[token_count:].reshape(-1)[: experts * token_count]
    by_expert = by_expert.reshape(experts, token_count)
    gate_grad = jnp.sum(jnp.where(hit, by_expert.T[:, None, :], 0.0), axis=2)

    hot = hot_slot[0]
    is_mine = hot % 2 == c
    flags = jnp.stack([hot // 2 == x, is_mine, c == 1]).astype(jnp.int32)
    def pick(piece, other):
        size = piece.shape[0] // 2
        part_own = lax.dynamic_slice_in_dim(piece, c * size, size, 0)
        part_other = lax.dynamic_slice_in_dim(other, c * size, size, 0)
        return jnp.where(is_mine, part_own, part_other)

    other_0, other_1 = grid.cross_core(new_0), grid.cross_core(new_1)
    direct_0, picked = stage(grid.cross_side(pick(new_0, other_0)), pick(new_1, other_1))
    direct_1 = grid.cross_side(picked)
    hot_copy = place_hot(0, flags, new_0, other_0, direct_0, grid.cross_core(direct_0), None)
    hot_copy, direct_1 = stage(hot_copy, direct_1)
    hot_copy = place_hot(1, flags, new_1, other_1, direct_1, grid.cross_core(direct_1), hot_copy)

    new_weights = full
    return (mixed, input_grad, gate_grad, new_weights[None], hot_copy[None])


def solution(mesh):
    return jax.shard_map(
        shards,
        mesh=mesh,
        in_specs=(
            P(BOTH, None),
            P(BOTH, None),
            P(BOTH, None),
            P(BOTH, None),
            P(BOTH, None, None),
            P(BOTH, None, None),
            P(BOTH, None, None),
            P("expert"),
        ),
        out_specs=(
            P(BOTH, None),
            P(BOTH, None),
            P(BOTH, None),
            P(BOTH, None, None),
            P(BOTH, None, None),
        ),
        check_vma=False,
    )
```

```python
import jax
import jax.numpy as jnp
from jax import lax
from jax.experimental import pallas as pl
from jax.experimental.pallas import tpu as pltpu
from jax.sharding import PartitionSpec as P

beta_first = 0.9
beta_second = 0.95
adam_eps = 1e-08
rate = 0.05
clip_norm = 1.0
bias_first = 1.0 - 0.9**10
bias_second = 1.0 - 0.95**10
BOTH = ("expert", "replica")
F32 = jnp.float32
BF16 = jnp.bfloat16
EXTRA = 8
BRIEF = pl.CostEstimate(flops=1, transcendentals=0, bytes_accessed=1)


class Grid:
    def __init__(self, groups, owners):
        self.line = groups // 2
        self.sides = owners // 2
        self.owners = owners
        self.count = groups * owners

    def split(self, device):
        place, owner = device // self.owners, device % self.owners
        return place // 2, place % 2, owner // 2, owner % 2

    def join(self, line, row, side, core):
        return ((line * 2 + row) * self.sides + side) * 2 + core

    def move(self, value, step):
        pairs = [(d, self.join(*step(*self.split(d)))) for d in range(self.count)]
        return lax.ppermute(value, BOTH, pairs)

    def up(self, value):
        return self.move(value, lambda z, y, x, c: ((z + 1) % self.line, y, x, c))

    def down(self, value):
        return self.move(value, lambda z, y, x, c: ((z - 1) % self.line, y, x, c))

    def cross_a(self, value):
        return self.move(value, lambda z, y, x, c: (z, y ^ (1 - c), x ^ c, c))

    def cross_b(self, value):
        return self.move(value, lambda z, y, x, c: (z, y ^ c, x ^ (1 - c), c))

    def cross_side(self, value):
        return self.move(value, lambda z, y, x, c: (z, y, x ^ 1, c))

    def cross_core(self, value):
        return self.move(value, lambda z, y, x, c: (z, y, x, c ^ 1))


NT = (((1,), (1,)), ((), ()))
TN = (((0,), (0,)), ((), ()))


def dot(a, b, dims=(((1,), (0,)), ((), ()))):
    return lax.dot_general(a, b, dims, preferred_element_type=F32)


def chunk_body(step, room, token_count, width, *refs):
    spot, tok_near, tok_far, cot_near, cot_far, select, select_t, gate, w_own, w_other = refs[:10]
    refs = refs[10 + (4 if step else 0) :]
    near_out, far_out = refs[:2]
    kept_out = refs[2:6]
    w, rows, cots, both, hidden, y, dx, dots, sem_w, sem_k = refs[6:]
    loads = [pltpu.make_async_copy(ref, w.at[e], sem_w.at[e]) for e, ref in enumerate((w_own, w_other))]
    for load in loads:
        load.start()
    near_far = ((tok_near, tok_far, rows), (cot_near, cot_far, cots))
    for near, far, out in near_far:
        for q in range(4):
            block = (near, near, far, far)[q][(q % 2) * token_count : (q % 2 + 1) * token_count, :]
            taken = dot(select[q], block).astype(BF16)
            for e in range(2):
                out[e, q * room : (q + 1) * room, :] = taken[e * room : (e + 1) * room]
    saves = []
    for e in range(2):
        loads[e].wait()
        gate_up = dot(rows[e], w[e, :, : 2 * width])
        spread = dot(cots[e], w[e, :, 2 * width :])
        gate_in, up_in = gate_up[:, :width], gate_up[:, width:]
        sig = jax.nn.sigmoid(gate_in)
        active = gate_in * sig
        hid = active * up_in
        products = jnp.sum(hid * spread, axis=1, keepdims=True)
        row_gates = []
        for q in range(4):
            chosen = select[q, e * room : (e + 1) * room, :].astype(F32)
            row_gates.append(jnp.sum(chosen * gate[q, e : e + 1, :], axis=1, keepdims=True))
            dots[q, e : e + 1, :] = jnp.sum(
                chosen * products[q * room : (q + 1) * room], axis=0, keepdims=True
            )
        row_gate = jnp.concatenate(row_gates, axis=0)
        hidden[e] = (hid * row_gate).astype(BF16)
        grad = spread * row_gate
        both[e, :, :width] = (grad * up_in * sig * (1.0 + gate_in * (1.0 - sig))).astype(BF16)
        both[e, :, width:] = (grad * active).astype(BF16)
        for i, (src, out) in enumerate(zip((rows, cots, both, hidden), kept_out)):
            save = pltpu.make_async_copy(src.at[e], out.at[step, e], sem_k.at[i, e])
            save.start()
            saves.append(save)
        out_y = dot(hidden[e], w[e, :, 2 * width :], NT).astype(BF16)
        out_dx = dot(both[e], w[e, :, : 2 * width], NT).astype(BF16)
        for q in range(4):
            y[q, e * room : (e + 1) * room, :] = out_y[q * room : (q + 1) * room]
            dx[q, e * room : (e + 1) * room, :] = out_dx[q * room : (q + 1) * room]
    model = near_out.shape[1]
    full_at = pl.multiple_of(spot[3] * room, room)
    rest_at = pl.multiple_of((1 - spot[3]) * room, room)
    for q in range(4):
        far = q > 1
        out = far_out if far else near_out
        size = room + room // 2 if far else token_count
        lines = size + EXTRA
        for src, start in ((y, (q % 2) * lines), (dx, 2 * lines + (q % 2) * size)):
            if far:
                out[start : start + room, :] = src[q, pl.ds(full_at, room), :]
                out[start + room : start + size, :] = src[q, pl.ds(rest_at, room // 2), :]
            else:
                out[start : start + size, :] = dot(select_t[q], src[q]).astype(BF16)
        pair = [dots[q, e : e + 1, :] for e in range(2)]
        even = jnp.where(spot[2] == 0, pair[0], pair[1])
        odd = jnp.where(spot[2] == 0, pair[1], pair[0])
        tiled = jnp.concatenate([even, odd] * (model // (2 * token_count)), axis=1)
        at_row = lax.broadcasted_iota(jnp.int32, (EXTRA, model), 0) == spot[0]
        at_lane = lax.broadcasted_iota(jnp.int32, (EXTRA, model), 1) // (2 * token_count) == spot[1]
        start = (q % 2) * lines + size
        out[start : start + EXTRA, :] = jnp.where(at_row & at_lane, tiled, 0.0).astype(BF16)
    for save in saves:
        save.wait()


def chunk(step, line, spot, blocks, select, select_t, gate, weights, kept, width):
    model = weights[0].shape[0]
    room, token_count = select.shape[1] // 2, select.shape[2]
    rows = 4 * room
    vmem = pl.BlockSpec(memory_space=pltpu.VMEM)
    hbm = pl.BlockSpec(memory_space=pl.ANY)
    near = jax.ShapeDtypeStruct((4 * token_count + 2 * EXTRA, model), BF16)
    far = jax.ShapeDtypeStruct((6 * room + 2 * EXTRA, model), BF16)
    sizes = (model, model, 2 * width, width)
    outs = (
        [near, far]
        + [jax.ShapeDtypeStruct((line, 2, rows, n), BF16) for n in sizes]
    )

    def body(*refs):
        chunk_body(step, room, token_count, width, *refs)

    result = pl.pallas_call(
        body,
        out_shape=outs,
        in_specs=[pl.BlockSpec(memory_space=pltpu.SMEM)]
        + [vmem] * 7
        + [hbm] * (2 + (4 if step else 0)),
        out_specs=[vmem] * 2 + [hbm] * 4,
        scratch_shapes=[pltpu.VMEM((2, model, 3 * width), BF16)]
        + [pltpu.VMEM((2, rows, n), BF16) for n in sizes]
        + [pltpu.VMEM((4, 2 * room, model), BF16)] * 2
        + [pltpu.VMEM((4, 2, token_count), F32)]
        + [pltpu.SemaphoreType.DMA((2,)), pltpu.SemaphoreType.DMA((4, 2))],
        input_output_aliases={10 + i: 2 + i for i in range(4)} if step else {},
        compiler_params=pltpu.CompilerParams(vmem_limit_bytes=56 * 1024 * 1024),
        cost_estimate=BRIEF,
        name="chunk",
    )(spot, *blocks, select, select_t, gate, *weights, *(kept if step else []))
    return result[:2], result[2:]


def weight_grad(kept, expert, block_rows=512):
    rows, cots, both, hidden = kept
    line, _, count, model = rows.shape
    width = hidden.shape[3]

    def body(rows, cots, both, hidden, out):
        flat = [ref[...].reshape(line * count, ref.shape[3]) for ref in (rows, cots, both, hidden)]
        out[:, : 2 * width] = dot(flat[0], flat[2], TN).astype(BF16)
        out[:, 2 * width :] = dot(flat[1], flat[3], TN).astype(BF16)

    part = pl.BlockSpec((line, 1, count, block_rows), lambda i: (0, expert, 0, i))

    def whole(n):
        return pl.BlockSpec((line, 1, count, n), lambda i: (0, expert, 0, 0))

    return pl.pallas_call(
        body,
        grid=(model // block_rows,),
        out_shape=jax.ShapeDtypeStruct((model, 3 * width), BF16),
        in_specs=[part, part, whole(2 * width), whole(width)],
        out_specs=pl.BlockSpec((block_rows, 3 * width), lambda i: (i, 0)),
        compiler_params=pltpu.CompilerParams(vmem_limit_bytes=56 * 1024 * 1024),
        cost_estimate=BRIEF,
        name="weight_grad",
    )(rows, cots, both, hidden)


def clip_factor(mine, received, clip_bound, block_rows=512):
    model, columns = mine.shape
    count = model // block_rows

    def body(mine, received, out, squares):
        step = pl.program_id(0)

        @pl.when(step == 0)
        def _():
            squares[...] = jnp.zeros_like(squares)

        def add_rows(i, total):
            at = pl.ds(pl.multiple_of(i * 16, 16), 16)
            g = mine[at, :].astype(F32) + received[at, :].astype(F32)
            return total + jnp.sum((g * g).reshape(2, 8, columns), axis=0)

        squares[...] = lax.fori_loop(0, block_rows // 16, add_rows, squares[...], unroll=2)

        @pl.when(step == count - 1)
        def _():
            norm = jnp.sqrt(jnp.sum(squares[...], axis=(0, 1), keepdims=True))
            out[...] = jnp.broadcast_to(jnp.minimum(1.0, clip_bound / (norm + 1e-06)), out.shape)

    block = pl.BlockSpec((block_rows, columns), lambda i: (i, 0))
    return pl.pallas_call(
        body,
        grid=(count,),
        out_shape=jax.ShapeDtypeStruct((8, 128), F32),
        in_specs=[block, block],
        out_specs=pl.BlockSpec((8, 128), lambda i: (0, 0)),
        scratch_shapes=[pltpu.VMEM((8, columns), F32)],
        cost_estimate=BRIEF,
        name="clip_factor",
    )(mine, received)


def adam(half, factor, mine, received, weights, moment_first, moment_second, full, block_rows=256):
    model, columns = weights.shape
    count = model // 2 // block_rows

    def body(factor, mine, received, w, m, v, *refs):
        full, piece = refs[-2:]
        scale = factor[0:1, 0:1]

        def update_rows(i, carry):
            at = pl.ds(pl.multiple_of(i * 16, 16), 16)
            scaled = scale * (mine[at, :].astype(F32) + received[at, :].astype(F32))
            first = beta_first * m[at, :].astype(F32) + (1.0 - beta_first) * scaled
            second = beta_second * v[at, :].astype(F32) + (1.0 - beta_second) * scaled * scaled
            root = jnp.sqrt(second * (1.0 / bias_second)) + adam_eps
            value = (w[at, :].astype(F32) - (rate / bias_first) * first / root).astype(BF16)
            full[at, :] = value
            piece[at, :] = value
            return carry

        lax.fori_loop(0, block_rows // 16, update_rows, 0)

    block = pl.BlockSpec((block_rows, columns), lambda i: (half * count + i, 0))
    given = [] if full is None else [full]
    return pl.pallas_call(
        body,
        grid=(count,),
        out_shape=[
            jax.ShapeDtypeStruct((model, columns), BF16),
            jax.ShapeDtypeStruct((model // 2, columns), BF16),
        ],
        in_specs=[pl.BlockSpec((8, 128), lambda i: (0, 0))]
        + [block] * 5
        + [pl.BlockSpec(memory_space=pl.ANY)] * len(given),
        out_specs=[block, pl.BlockSpec((block_rows, columns), lambda i: (i, 0))],
        input_output_aliases={6: 0} if given else {},
        cost_estimate=BRIEF,
        name="adam",
    )(factor, mine, received, weights, moment_first, moment_second, *given)


def place_hot(half, flags, own, other, direct, relayed, full):
    rows, columns = own.shape
    block_rows = rows // 4
    spot = jax.ShapeDtypeStruct((2 * rows, columns), BF16)

    def body(flags, own, other, direct, relayed, *refs):
        here, mine = flags[0] == 1, flags[1] == 1
        first = (pl.program_id(0) < 2) == (flags[2] == 0)
        for wanted, ref in (
            (here & mine, own),
            (here & ~mine, other),
            (~here & first, direct),
            (~here & ~first, relayed),
        ):

            @pl.when(wanted)
            def _(ref=ref):
                refs[-1][...] = ref[...]

    def spec(where):
        return pl.BlockSpec((block_rows, columns), lambda i, flags: (where(i, flags), 0))

    given = [] if full is None else [full]
    return pl.pallas_call(
        body,
        out_shape=spot,
        grid_spec=pltpu.PrefetchScalarGridSpec(
            num_scalar_prefetch=1,
            grid=(4,),
            in_specs=[
                spec(lambda i, f: i * f[0] * f[1]),
                spec(lambda i, f: i * f[0] * (1 - f[1])),
                spec(lambda i, f: (1 - f[0]) * jnp.clip(i - 2 * f[2], 0, 1)),
                spec(lambda i, f: (1 - f[0]) * jnp.clip(i - 2 * (1 - f[2]), 0, 1)),
            ]
            + [pl.BlockSpec(memory_space=pl.ANY)] * len(given),
            out_specs=spec(lambda i, f: 4 * half + i),
        ),
        input_output_aliases={5: 0} if given else {},
        cost_estimate=BRIEF,
        name="place_hot",
    )(flags, own, other, direct, relayed, *given)


def combine(near, back, expand, before, last):
    rows, columns = near.shape
    n = (rows - 2 * EXTRA) // 4
    m, k = n + EXTRA, expand.shape[2]
    width = columns // 2
    up_rows = m if last else (2 * n if before is None else 2 * n + m)
    sizes = [m, m + n if last else m, up_rows] + ([n] if last else [])

    def body(*refs):
        given, outs = refs[: -len(sizes)], refs[-len(sizes) :]
        own, across, up = outs[:3]
        near, back, expand = given[:3]

        def plain(at, came):
            return near[at : at + EXTRA, :].astype(F32) + back[came : came + EXTRA, :].astype(F32)

        def part(i, at, came):
            return near[at : at + n, :].astype(F32) + dot(expand[i], back[came : came + k, :])

        for i, out in enumerate((own, across)):
            out[:n, :] = part(i, i * m, i * (k + EXTRA)).astype(BF16)
            out[n:m, :] = plain(i * m + n, i * (k + EXTRA) + k).astype(BF16)
        came = 2 * (k + EXTRA)
        grads = jnp.concatenate([part(i, 2 * m + i * n, came + i * k) for i in range(2)])
        if before is not None:
            old_own, old_across, old_up = given[3:]
            grads = grads + old_up[: 2 * n, :].astype(F32)
            waiting = old_own[...].astype(F32) + old_across[...].astype(F32)
            if before[2].shape[0] > 2 * n:
                waiting = waiting + old_up[2 * n :, :].astype(F32)
            up[up_rows - m :, :] = waiting.astype(BF16)
        if last:
            outs[3][...] = grads[:n].astype(BF16)
            across[m:, :] = grads[n:].astype(BF16)
        else:
            up[: 2 * n, :] = grads.astype(BF16)

    given = [near, back, expand] + ([] if before is None else list(before))
    return pl.pallas_call(
        body,
        grid=(2,),
        out_shape=[jax.ShapeDtypeStruct((size, columns), BF16) for size in sizes],
        in_specs=[
            pl.BlockSpec(v.shape, lambda i: (0, 0, 0))
            if v is expand
            else pl.BlockSpec((v.shape[0], width), lambda i: (0, i))
            for v in given
        ],
        out_specs=[pl.BlockSpec((size, width), lambda i: (0, i)) for size in sizes],
        compiler_params=pltpu.CompilerParams(vmem_limit_bytes=56 * 1024 * 1024),
        cost_estimate=BRIEF,
        name="combine",
    )(*given)


def stage(*values):
    return lax.optimization_barrier(values)


def add(*values):
    total = values[0].astype(F32)
    for value in values[1:]:
        total = total + value.astype(F32)
    return total


def shards(
    tokens, expert_ids, gates, cotangent, expert_weights, moment_first, moment_second, hot_slot
):
    groups = lax.axis_size("expert")
    owners = lax.axis_size("replica")
    experts = groups * owners
    grid = Grid(groups, owners)
    line = grid.line
    token_count, chosen = expert_ids.shape
    width = expert_weights.shape[2] // 3
    room = 2 * token_count * chosen // experts
    device = lax.axis_index("expert") * owners + lax.axis_index("replica")
    z, y, x, c = grid.split(device)
    weights = expert_weights[0]

    expert_range = jnp.arange(experts, dtype=jnp.int32)
    hit = expert_ids[:, :, None] == expert_range
    gate_table = jnp.sum(jnp.where(hit, gates[:, :, None], 0.0), axis=1).T
    places = [grid.split(d) for d in range(experts)]
    met = [
        d // 2 * 2 + e for d in range(experts) for e in range(2)
    ], [
        grid.join(pz, py ^ pc, px ^ (1 - pc), 0) + e for pz, py, px, pc in places for e in range(2)
    ]
    wanted = jnp.array(met, jnp.int32).reshape(2, experts, 2).transpose(1, 0, 2).reshape(-1)
    table = lax.all_to_all(
        gate_table[wanted].reshape(experts, 4 * token_count),
        BOTH,
        split_axis=0,
        concat_axis=0,
        tiled=True,
    ).reshape(experts, 4, token_count)

    def route(table):
        steps = jnp.arange(line, dtype=jnp.int32)[:, None]
        flip_a = jnp.array([0, 1, 0, 1], jnp.int32)[None]
        flip_b = jnp.array([0, 0, 1, 1], jnp.int32)[None]
        flip_y = jnp.where(c == 0, flip_a, flip_b)
        flip_x = jnp.where(c == 0, flip_b, flip_a)
        source = grid.join((z - steps) % line, y ^ flip_y, x ^ flip_x, c)
        gate_slot = table[source][:, :, :2]
        gate_slot = jnp.where(c == 0, gate_slot, gate_slot[:, :, ::-1])
        taken = gate_slot > 0.0
        before = jnp.triu(jnp.ones((token_count, token_count), BF16), 1)
        ahead = jnp.dot(taken.astype(BF16), before, preferred_element_type=F32).astype(jnp.int32)
        slot = jnp.where(taken, ahead, room)
        places = jnp.arange(room, dtype=jnp.int32)
        select = (slot[:, :, :, None, :] == places[:, None]).astype(BF16)
        select = select.reshape(line, 4, 2 * room, token_count)
        select_t = (slot.transpose(0, 1, 3, 2)[..., None] == places).astype(BF16)
        select_t = select_t.reshape(line, 4, token_count, 2 * room)
        counts = jnp.sum((table[source[0, 0]] > 0.0).astype(jnp.int32), axis=1)
        fuller = (counts[1::2] > room // 2).astype(jnp.int32)
        there = table[source[:, :2]][:, :, 2:]
        there = jnp.where(fuller[1] == 1, there[:, :, ::-1], there) > 0.0
        spread = jnp.dot(there.astype(BF16), before, preferred_element_type=F32).astype(jnp.int32)
        spread = jnp.where(there, spread, room).transpose(0, 1, 3, 2)[..., None]
        expand = jnp.concatenate(
            [spread[:, :, :, 0] == places, spread[:, :, :, 1] == places[: room // 2]], axis=3
        ).astype(BF16)
        here = jnp.where(fuller[0] == c, 0, 1)
        return select, select_t, gate_slot, expand, here

    per_row = expert_weights.shape[1] // (2 * token_count)
    chip = device // 2

    def run_chunk(r, kept):
        return chunk(r, line, spot, blocks[r], select[r], select_t[r], gate_slot[r], pair, kept, width)

    pair = (weights, grid.cross_core(weights))
    tok = (tokens, grid.up(tokens))
    tok_a, cot_near = stage(
        grid.cross_a(tokens), jnp.concatenate([cotangent, grid.cross_a(cotangent)])
    )
    tok = list(tok)
    blocks, parts, kept = [], [], []
    tok_near = jnp.concatenate([tok[0], tok_a])
    for r in range(line):
        far = (grid.cross_b(tok_near), grid.cross_b(cot_near))
        more = {}
        if r + 1 < line:
            more["cot"] = grid.up(cot_near)
            more["a"] = grid.cross_a(tok[r + 1])
        if r + 2 < line:
            more["tok"] = grid.up(tok[r + 1])
        done = None
        if r:
            done = run_chunk(r - 1, kept)
        ready = (tok_near, far[0], cot_near, far[1])
        if r == 0:
            ready, more, table, pair, tok = stage(ready, more, table, pair, tok)
            select, select_t, gate_slot, expand, here = route(table)
            spot = jnp.stack([chip // per_row, chip % per_row, c, here]).astype(jnp.int32)
        else:
            ready, more, done, parts = stage(ready, more, done, parts)
        blocks.append(list(ready))
        if done is not None:
            part, kept = done
            parts.append(part)
        if r + 1 < line:
            cot_near = more["cot"]
            tok_near = jnp.concatenate([tok[r + 1], more["a"]])
        if r + 2 < line:
            tok.append(more["tok"])

    order = list(range(1, line)) + [0]
    back = grid.cross_b(parts[order[0]][1])
    part, kept = run_chunk(line - 1, kept)
    back, part, kept, other_grad, parts = stage(back, part, kept, weight_grad(kept, 1), parts)
    back = {order[0]: back}
    parts.append(part)

    before = None
    for i, r in enumerate(order):
        last = i + 1 == line
        own, across, up, *dx_own = combine(parts[r][0], back[r], expand[r], before, last)
        moves = [grid.cross_a(across), grid.up(up)]
        coming = order[i + 1 : i + 2] if i != 1 else order[2:3] + order[-1:]
        coming = [n for n in coming if n not in back]
        more = [grid.cross_b(parts[n][1]) for n in coming]
        work = ()
        if i == 0:
            work = (grid.cross_core(other_grad), weight_grad(kept, 0))
        if i == 1:
            factor = clip_factor(mine, received, clip_norm * experts ** (-0.5))
            given = (factor, mine, received, weights, moment_first[0], moment_second[0])
            full, new_0 = adam(0, *given, None)
            full, new_1 = adam(1, *given, full)
            work = (full, new_0, new_1)
        moves, more, work, own, dx_own, parts = stage(moves, more, work, own, dx_own, parts)
        if i == 0:
            received, mine = work
        if i == 1:
            full, new_0, new_1 = work
        back.update(zip(coming, more))
        before = (own, *moves)
    total = add(own, moves[0][: token_count + EXTRA], moves[1])
    mixed = total[:token_count].astype(BF16)
    input_grad = add(dx_own[0], moves[0][token_count + EXTRA :]).astype(BF16)
    by_expert = total[token_count:].reshape(-1)[: experts * token_count]
    by_expert = by_expert.reshape(experts, token_count)
    gate_grad = jnp.sum(jnp.where(hit, by_expert.T[:, None, :], 0.0), axis=2)

    hot = hot_slot[0]
    is_mine = hot % 2 == c
    flags = jnp.stack([hot // 2 == x, is_mine, c == 1]).astype(jnp.int32)
    def pick(piece, other):
        size = piece.shape[0] // 2
        part_own = lax.dynamic_slice_in_dim(piece, c * size, size, 0)
        part_other = lax.dynamic_slice_in_dim(other, c * size, size, 0)
        return jnp.where(is_mine, part_own, part_other)

    other_0, other_1 = grid.cross_core(new_0), grid.cross_core(new_1)
    direct_0, picked = stage(grid.cross_side(pick(new_0, other_0)), pick(new_1, other_1))
    direct_1 = grid.cross_side(picked)
    hot_copy = place_hot(0, flags, new_0, other_0, direct_0, grid.cross_core(direct_0), None)
    hot_copy, direct_1 = stage(hot_copy, direct_1)
    hot_copy = place_hot(1, flags, new_1, other_1, direct_1, grid.cross_core(direct_1), hot_copy)

    new_weights = full
    return (mixed, input_grad, gate_grad, new_weights[None], hot_copy[None])


def solution(mesh):
    return jax.shard_map(
        shards,
        mesh=mesh,
        in_specs=(
            P(BOTH, None),
            P(BOTH, None),
            P(BOTH, None),
            P(BOTH, None),
            P(BOTH, None, None),
            P(BOTH, None, None),
            P(BOTH, None, None),
            P("expert"),
        ),
        out_specs=(
            P(BOTH, None),
            P(BOTH, None),
            P(BOTH, None),
            P(BOTH, None, None),
            P(BOTH, None, None),
        ),
        check_vma=False,
    )
```

```python
import jax
import jax.numpy as jnp
from jax import lax
from jax.experimental import pallas as pl
from jax.experimental.pallas import tpu as pltpu
from jax.sharding import PartitionSpec as P

beta_first = 0.9
beta_second = 0.95
adam_eps = 1e-08
rate = 0.05
clip_norm = 1.0
bias_first = 1.0 - 0.9**10
bias_second = 1.0 - 0.95**10
BOTH = ("expert", "replica")
F32 = jnp.float32
BF16 = jnp.bfloat16
EXTRA = 8
BRIEF = pl.CostEstimate(flops=1, transcendentals=0, bytes_accessed=1)


class Grid:
    def __init__(self, groups, owners):
        self.line = groups // 2
        self.sides = owners // 2
        self.owners = owners
        self.count = groups * owners

    def split(self, device):
        place, owner = device // self.owners, device % self.owners
        return place // 2, place % 2, owner // 2, owner % 2

    def join(self, line, row, side, core):
        return ((line * 2 + row) * self.sides + side) * 2 + core

    def move(self, value, step):
        pairs = [(d, self.join(*step(*self.split(d)))) for d in range(self.count)]
        return lax.ppermute(value, BOTH, pairs)

    def up(self, value):
        return self.move(value, lambda z, y, x, c: ((z + 1) % self.line, y, x, c))

    def down(self, value):
        return self.move(value, lambda z, y, x, c: ((z - 1) % self.line, y, x, c))

    def cross_a(self, value):
        return self.move(value, lambda z, y, x, c: (z, y ^ (1 - c), x ^ c, c))

    def cross_b(self, value):
        return self.move(value, lambda z, y, x, c: (z, y ^ c, x ^ (1 - c), c))

    def cross_side(self, value):
        return self.move(value, lambda z, y, x, c: (z, y, x ^ 1, c))

    def cross_core(self, value):
        return self.move(value, lambda z, y, x, c: (z, y, x, c ^ 1))


NT = (((1,), (1,)), ((), ()))
TN = (((0,), (0,)), ((), ()))


def dot(a, b, dims=(((1,), (0,)), ((), ()))):
    return lax.dot_general(a, b, dims, preferred_element_type=F32)


def chunk_body(step, room, token_count, width, *refs):
    spot, tok_near, tok_far, cot_near, cot_far, select, select_t, gate, w_own, w_other = refs[:10]
    refs = refs[10 + (4 if step else 0) :]
    near_out, far_out = refs[:2]
    kept_out = refs[2:6]
    w, rows, cots, both, hidden, y, dx, dots, sem_w, sem_k = refs[6:]
    loads = [pltpu.make_async_copy(ref, w.at[e], sem_w.at[e]) for e, ref in enumerate((w_own, w_other))]
    for load in loads:
        load.start()
    near_far = ((tok_near, tok_far, rows), (cot_near, cot_far, cots))
    for near, far, out in near_far:
        for q in range(4):
            block = (near, near, far, far)[q][(q % 2) * token_count : (q % 2 + 1) * token_count, :]
            taken = dot(select[q], block).astype(BF16)
            for e in range(2):
                out[e, q * room : (q + 1) * room, :] = taken[e * room : (e + 1) * room]
    saves = []
    for e in range(2):
        loads[e].wait()
        gate_up = dot(rows[e], w[e, :, : 2 * width])
        spread = dot(cots[e], w[e, :, 2 * width :])
        gate_in, up_in = gate_up[:, :width], gate_up[:, width:]
        sig = jax.nn.sigmoid(gate_in)
        active = gate_in * sig
        hid = active * up_in
        products = jnp.sum(hid * spread, axis=1, keepdims=True)
        row_gates = []
        for q in range(4):
            chosen = select[q, e * room : (e + 1) * room, :].astype(F32)
            row_gates.append(jnp.sum(chosen * gate[q, e : e + 1, :], axis=1, keepdims=True))
            dots[q, e : e + 1, :] = jnp.sum(
                chosen * products[q * room : (q + 1) * room], axis=0, keepdims=True
            )
        row_gate = jnp.concatenate(row_gates, axis=0)
        hidden[e] = (hid * row_gate).astype(BF16)
        grad = spread * row_gate
        both[e, :, :width] = (grad * up_in * sig * (1.0 + gate_in * (1.0 - sig))).astype(BF16)
        both[e, :, width:] = (grad * active).astype(BF16)
        for i, (src, out) in enumerate(zip((rows, cots, both, hidden), kept_out)):
            save = pltpu.make_async_copy(src.at[e], out.at[step, e], sem_k.at[i, e])
            save.start()
            saves.append(save)
        out_y = dot(hidden[e], w[e, :, 2 * width :], NT).astype(BF16)
        out_dx = dot(both[e], w[e, :, : 2 * width], NT).astype(BF16)
        for q in range(4):
            y[q, e * room : (e + 1) * room, :] = out_y[q * room : (q + 1) * room]
            dx[q, e * room : (e + 1) * room, :] = out_dx[q * room : (q + 1) * room]
    model = near_out.shape[1]
    full_at = pl.multiple_of(spot[3] * room, room)
    rest_at = pl.multiple_of((1 - spot[3]) * room, room)
    for q in range(4):
        far = q > 1
        out = far_out if far else near_out
        size = room + room // 2 if far else token_count
        lines = size + EXTRA
        for src, start in ((y, (q % 2) * lines), (dx, 2 * lines + (q % 2) * size)):
            if far:
                out[start : start + room, :] = src[q, pl.ds(full_at, room), :]
                out[start + room : start + size, :] = src[q, pl.ds(rest_at, room // 2), :]
            else:
                out[start : start + size, :] = dot(select_t[q], src[q]).astype(BF16)
        pair = [dots[q, e : e + 1, :] for e in range(2)]
        even = jnp.where(spot[2] == 0, pair[0], pair[1])
        odd = jnp.where(spot[2] == 0, pair[1], pair[0])
        tiled = jnp.concatenate([even, odd] * (model // (2 * token_count)), axis=1)
        at_row = lax.broadcasted_iota(jnp.int32, (EXTRA, model), 0) == spot[0]
        at_lane = lax.broadcasted_iota(jnp.int32, (EXTRA, model), 1) // (2 * token_count) == spot[1]
        start = (q % 2) * lines + size
        out[start : start + EXTRA, :] = jnp.where(at_row & at_lane, tiled, 0.0).astype(BF16)
    for save in saves:
        save.wait()


def chunk(step, line, spot, blocks, select, select_t, gate, weights, kept, width):
    model = weights[0].shape[0]
    room, token_count = select.shape[1] // 2, select.shape[2]
    rows = 4 * room
    vmem = pl.BlockSpec(memory_space=pltpu.VMEM)
    hbm = pl.BlockSpec(memory_space=pl.ANY)
    near = jax.ShapeDtypeStruct((4 * token_count + 2 * EXTRA, model), BF16)
    far = jax.ShapeDtypeStruct((6 * room + 2 * EXTRA, model), BF16)
    sizes = (model, model, 2 * width, width)
    outs = (
        [near, far]
        + [jax.ShapeDtypeStruct((line, 2, rows, n), BF16) for n in sizes]
    )

    def body(*refs):
        chunk_body(step, room, token_count, width, *refs)

    result = pl.pallas_call(
        body,
        out_shape=outs,
        in_specs=[pl.BlockSpec(memory_space=pltpu.SMEM)]
        + [vmem] * 7
        + [hbm] * (2 + (4 if step else 0)),
        out_specs=[vmem] * 2 + [hbm] * 4,
        scratch_shapes=[pltpu.VMEM((2, model, 3 * width), BF16)]
        + [pltpu.VMEM((2, rows, n), BF16) for n in sizes]
        + [pltpu.VMEM((4, 2 * room, model), BF16)] * 2
        + [pltpu.VMEM((4, 2, token_count), F32)]
        + [pltpu.SemaphoreType.DMA((2,)), pltpu.SemaphoreType.DMA((4, 2))],
        input_output_aliases={10 + i: 2 + i for i in range(4)} if step else {},
        compiler_params=pltpu.CompilerParams(vmem_limit_bytes=56 * 1024 * 1024),
        cost_estimate=BRIEF,
        name="chunk",
    )(spot, *blocks, select, select_t, gate, *weights, *(kept if step else []))
    return result[:2], result[2:]


def weight_grad(kept, expert, block_rows=512):
    rows, cots, both, hidden = kept
    line, _, count, model = rows.shape
    width = hidden.shape[3]

    def body(rows, cots, both, hidden, out):
        flat = [ref[...].reshape(line * count, ref.shape[3]) for ref in (rows, cots, both, hidden)]
        out[:, : 2 * width] = dot(flat[0], flat[2], TN).astype(BF16)
        out[:, 2 * width :] = dot(flat[1], flat[3], TN).astype(BF16)

    part = pl.BlockSpec((line, 1, count, block_rows), lambda i: (0, expert, 0, i))

    def whole(n):
        return pl.BlockSpec((line, 1, count, n), lambda i: (0, expert, 0, 0))

    return pl.pallas_call(
        body,
        grid=(model // block_rows,),
        out_shape=jax.ShapeDtypeStruct((model, 3 * width), BF16),
        in_specs=[part, part, whole(2 * width), whole(width)],
        out_specs=pl.BlockSpec((block_rows, 3 * width), lambda i: (i, 0)),
        compiler_params=pltpu.CompilerParams(vmem_limit_bytes=56 * 1024 * 1024),
        cost_estimate=BRIEF,
        name="weight_grad",
    )(rows, cots, both, hidden)


def clip_factor(mine, received, clip_bound, block_rows=512):
    model, columns = mine.shape
    count = model // block_rows

    def body(mine, received, out, squares):
        step = pl.program_id(0)

        @pl.when(step == 0)
        def _():
            squares[...] = jnp.zeros_like(squares)

        def add_rows(i, total):
            at = pl.ds(pl.multiple_of(i * 16, 16), 16)
            g = mine[at, :].astype(F32) + received[at, :].astype(F32)
            return total + jnp.sum((g * g).reshape(2, 8, columns), axis=0)

        squares[...] = lax.fori_loop(0, block_rows // 16, add_rows, squares[...], unroll=2)

        @pl.when(step == count - 1)
        def _():
            norm = jnp.sqrt(jnp.sum(squares[...], axis=(0, 1), keepdims=True))
            out[...] = jnp.broadcast_to(jnp.minimum(1.0, clip_bound / (norm + 1e-06)), out.shape)

    block = pl.BlockSpec((block_rows, columns), lambda i: (i, 0))
    return pl.pallas_call(
        body,
        grid=(count,),
        out_shape=jax.ShapeDtypeStruct((8, 128), F32),
        in_specs=[block, block],
        out_specs=pl.BlockSpec((8, 128), lambda i: (0, 0)),
        scratch_shapes=[pltpu.VMEM((8, columns), F32)],
        cost_estimate=BRIEF,
        name="clip_factor",
    )(mine, received)


def adam(half, factor, mine, received, weights, moment_first, moment_second, full, block_rows=256):
    model, columns = weights.shape
    count = model // 2 // block_rows

    def body(factor, mine, received, w, m, v, *refs):
        full, piece = refs[-2:]
        scale = factor[0:1, 0:1]

        def update_rows(i, carry):
            at = pl.ds(pl.multiple_of(i * 16, 16), 16)
            scaled = scale * (mine[at, :].astype(F32) + received[at, :].astype(F32))
            first = beta_first * m[at, :].astype(F32) + (1.0 - beta_first) * scaled
            second = beta_second * v[at, :].astype(F32) + (1.0 - beta_second) * scaled * scaled
            root = jnp.sqrt(second * (1.0 / bias_second)) + adam_eps
            value = (w[at, :].astype(F32) - (rate / bias_first) * first / root).astype(BF16)
            full[at, :] = value
            piece[at, :] = value
            return carry

        lax.fori_loop(0, block_rows // 16, update_rows, 0)

    block = pl.BlockSpec((block_rows, columns), lambda i: (half * count + i, 0))
    given = [] if full is None else [full]
    return pl.pallas_call(
        body,
        grid=(count,),
        out_shape=[
            jax.ShapeDtypeStruct((model, columns), BF16),
            jax.ShapeDtypeStruct((model // 2, columns), BF16),
        ],
        in_specs=[pl.BlockSpec((8, 128), lambda i: (0, 0))]
        + [block] * 5
        + [pl.BlockSpec(memory_space=pl.ANY)] * len(given),
        out_specs=[block, pl.BlockSpec((block_rows, columns), lambda i: (i, 0))],
        input_output_aliases={6: 0} if given else {},
        cost_estimate=BRIEF,
        name="adam",
    )(factor, mine, received, weights, moment_first, moment_second, *given)


def place_hot(half, flags, own, other, direct, relayed, full):
    rows, columns = own.shape
    block_rows = rows // 4
    spot = jax.ShapeDtypeStruct((2 * rows, columns), BF16)

    def body(flags, own, other, direct, relayed, *refs):
        here, mine = flags[0] == 1, flags[1] == 1
        first = (pl.program_id(0) < 2) == (flags[2] == 0)
        for wanted, ref in (
            (here & mine, own),
            (here & ~mine, other),
            (~here & first, direct),
            (~here & ~first, relayed),
        ):

            @pl.when(wanted)
            def _(ref=ref):
                refs[-1][...] = ref[...]

    def spec(where):
        return pl.BlockSpec((block_rows, columns), lambda i, flags: (where(i, flags), 0))

    given = [] if full is None else [full]
    return pl.pallas_call(
        body,
        out_shape=spot,
        grid_spec=pltpu.PrefetchScalarGridSpec(
            num_scalar_prefetch=1,
            grid=(4,),
            in_specs=[
                spec(lambda i, f: i * f[0] * f[1]),
                spec(lambda i, f: i * f[0] * (1 - f[1])),
                spec(lambda i, f: (1 - f[0]) * jnp.clip(i - 2 * f[2], 0, 1)),
                spec(lambda i, f: (1 - f[0]) * jnp.clip(i - 2 * (1 - f[2]), 0, 1)),
            ]
            + [pl.BlockSpec(memory_space=pl.ANY)] * len(given),
            out_specs=spec(lambda i, f: 4 * half + i),
        ),
        input_output_aliases={5: 0} if given else {},
        cost_estimate=BRIEF,
        name="place_hot",
    )(flags, own, other, direct, relayed, *given)


def combine(near, back, expand, before, last):
    rows, columns = near.shape
    n = (rows - 2 * EXTRA) // 4
    m, k = n + EXTRA, expand.shape[2]
    width = columns // 2
    up_rows = m if last else (2 * n if before is None else 2 * n + m)
    sizes = [m, m + n if last else m, up_rows] + ([n] if last else [])

    def body(*refs):
        given, outs = refs[: -len(sizes)], refs[-len(sizes) :]
        own, across, up = outs[:3]
        near, back, expand = given[:3]

        def plain(at, came):
            return near[at : at + EXTRA, :].astype(F32) + back[came : came + EXTRA, :].astype(F32)

        def part(i, at, came):
            return near[at : at + n, :].astype(F32) + dot(expand[i], back[came : came + k, :])

        for i, out in enumerate((own, across)):
            out[:n, :] = part(i, i * m, i * (k + EXTRA)).astype(BF16)
            out[n:m, :] = plain(i * m + n, i * (k + EXTRA) + k).astype(BF16)
        came = 2 * (k + EXTRA)
        grads = jnp.concatenate([part(i, 2 * m + i * n, came + i * k) for i in range(2)])
        if before is not None:
            old_own, old_across, old_up = given[3:]
            grads = grads + old_up[: 2 * n, :].astype(F32)
            waiting = old_own[...].astype(F32) + old_across[...].astype(F32)
            if before[2].shape[0] > 2 * n:
                waiting = waiting + old_up[2 * n :, :].astype(F32)
            up[up_rows - m :, :] = waiting.astype(BF16)
        if last:
            outs[3][...] = grads[:n].astype(BF16)
            across[m:, :] = grads[n:].astype(BF16)
        else:
            up[: 2 * n, :] = grads.astype(BF16)

    given = [near, back, expand] + ([] if before is None else list(before))
    return pl.pallas_call(
        body,
        grid=(2,),
        out_shape=[jax.ShapeDtypeStruct((size, columns), BF16) for size in sizes],
        in_specs=[
            pl.BlockSpec(v.shape, lambda i: (0, 0, 0))
            if v is expand
            else pl.BlockSpec((v.shape[0], width), lambda i: (0, i))
            for v in given
        ],
        out_specs=[pl.BlockSpec((size, width), lambda i: (0, i)) for size in sizes],
        compiler_params=pltpu.CompilerParams(vmem_limit_bytes=56 * 1024 * 1024),
        cost_estimate=BRIEF,
        name="combine",
    )(*given)


def stage(*values):
    return lax.optimization_barrier(values)


def add(*values):
    total = values[0].astype(F32)
    for value in values[1:]:
        total = total + value.astype(F32)
    return total


def shards(
    tokens, expert_ids, gates, cotangent, expert_weights, moment_first, moment_second, hot_slot
):
    groups = lax.axis_size("expert")
    owners = lax.axis_size("replica")
    experts = groups * owners
    grid = Grid(groups, owners)
    line = grid.line
    token_count, chosen = expert_ids.shape
    width = expert_weights.shape[2] // 3
    room = 2 * token_count * chosen // experts
    device = lax.axis_index("expert") * owners + lax.axis_index("replica")
    z, y, x, c = grid.split(device)
    weights = expert_weights[0]

    expert_range = jnp.arange(experts, dtype=jnp.int32)
    hit = expert_ids[:, :, None] == expert_range
    gate_table = jnp.sum(jnp.where(hit, gates[:, :, None], 0.0), axis=1).T
    places = [grid.split(d) for d in range(experts)]
    met = [
        d // 2 * 2 + e for d in range(experts) for e in range(2)
    ], [
        grid.join(pz, py ^ pc, px ^ (1 - pc), 0) + e for pz, py, px, pc in places for e in range(2)
    ]
    wanted = jnp.array(met, jnp.int32).reshape(2, experts, 2).transpose(1, 0, 2).reshape(-1)
    table = lax.all_to_all(
        gate_table[wanted].reshape(experts, 4 * token_count),
        BOTH,
        split_axis=0,
        concat_axis=0,
        tiled=True,
    ).reshape(experts, 4, token_count)

    def route(table):
        steps = jnp.arange(line, dtype=jnp.int32)[:, None]
        flip_a = jnp.array([0, 1, 0, 1], jnp.int32)[None]
        flip_b = jnp.array([0, 0, 1, 1], jnp.int32)[None]
        flip_y = jnp.where(c == 0, flip_a, flip_b)
        flip_x = jnp.where(c == 0, flip_b, flip_a)
        source = grid.join((z - steps) % line, y ^ flip_y, x ^ flip_x, c)
        gate_slot = table[source][:, :, :2]
        gate_slot = jnp.where(c == 0, gate_slot, gate_slot[:, :, ::-1])
        taken = gate_slot > 0.0
        before = jnp.triu(jnp.ones((token_count, token_count), BF16), 1)
        ahead = jnp.dot(taken.astype(BF16), before, preferred_element_type=F32).astype(jnp.int32)
        slot = jnp.where(taken, ahead, room)
        places = jnp.arange(room, dtype=jnp.int32)
        select = (slot[:, :, :, None, :] == places[:, None]).astype(BF16)
        select = select.reshape(line, 4, 2 * room, token_count)
        select_t = (slot.transpose(0, 1, 3, 2)[..., None] == places).astype(BF16)
        select_t = select_t.reshape(line, 4, token_count, 2 * room)
        counts = jnp.sum((table[source[0, 0]] > 0.0).astype(jnp.int32), axis=1)
        fuller = (counts[1::2] > room // 2).astype(jnp.int32)
        there = table[source[:, :2]][:, :, 2:]
        there = jnp.where(fuller[1] == 1, there[:, :, ::-1], there) > 0.0
        spread = jnp.dot(there.astype(BF16), before, preferred_element_type=F32).astype(jnp.int32)
        spread = jnp.where(there, spread, room).transpose(0, 1, 3, 2)[..., None]
        expand = jnp.concatenate(
            [spread[:, :, :, 0] == places, spread[:, :, :, 1] == places[: room // 2]], axis=3
        ).astype(BF16)
        here = jnp.where(fuller[0] == c, 0, 1)
        return select, select_t, gate_slot, [expand[r] for r in range(line)], here

    per_row = expert_weights.shape[1] // (2 * token_count)
    chip = device // 2

    def run_chunk(r, kept):
        return chunk(r, line, spot, blocks[r], select[r], select_t[r], gate_slot[r], pair, kept, width)

    pair = (weights, grid.cross_core(weights))
    tok = (tokens, grid.up(tokens))
    tok_a, cot_near = stage(
        grid.cross_a(tokens), jnp.concatenate([cotangent, grid.cross_a(cotangent)])
    )
    tok = list(tok)
    blocks, parts, kept = [], [], []
    tok_near = jnp.concatenate([tok[0], tok_a])
    for r in range(line):
        far = (grid.cross_b(tok_near), grid.cross_b(cot_near))
        more = {}
        if r + 1 < line:
            more["cot"] = grid.up(cot_near)
            more["a"] = grid.cross_a(tok[r + 1])
        if r + 2 < line:
            more["tok"] = grid.up(tok[r + 1])
        done = None
        if r:
            done = run_chunk(r - 1, kept)
        ready = (tok_near, far[0], cot_near, far[1])
        if r == 0:
            ready, more, table, pair, tok = stage(ready, more, table, pair, tok)
            select, select_t, gate_slot, expand, here = route(table)
            spot = jnp.stack([chip // per_row, chip % per_row, c, here]).astype(jnp.int32)
        else:
            ready, more, done, parts, expand = stage(ready, more, done, parts, expand)
        blocks.append(list(ready))
        if done is not None:
            part, kept = done
            parts.append(part)
        if r + 1 < line:
            cot_near = more["cot"]
            tok_near = jnp.concatenate([tok[r + 1], more["a"]])
        if r + 2 < line:
            tok.append(more["tok"])

    order = list(range(1, line)) + [0]
    back = grid.cross_b(parts[order[0]][1])
    part, kept = run_chunk(line - 1, kept)
    back, part, kept, other_grad, parts = stage(back, part, kept, weight_grad(kept, 1), parts)
    back = {order[0]: back}
    parts.append(part)

    before = None
    for i, r in enumerate(order):
        last = i + 1 == line
        own, across, up, *dx_own = combine(parts[r][0], back[r], expand[r], before, last)
        moves = [grid.cross_a(across), grid.up(up)]
        coming = order[i + 1 : i + 2] if i != 1 else order[2:3] + order[-1:]
        coming = [n for n in coming if n not in back]
        more = [grid.cross_b(parts[n][1]) for n in coming]
        work = ()
        if i == 0:
            work = (grid.cross_core(other_grad), weight_grad(kept, 0))
        if i == 1:
            factor = clip_factor(mine, received, clip_norm * experts ** (-0.5))
            given = (factor, mine, received, weights, moment_first[0], moment_second[0])
            full, new_0 = adam(0, *given, None)
            full, new_1 = adam(1, *given, full)
            work = (full, new_0, new_1)
        moves, more, work, own, dx_own, parts = stage(moves, more, work, own, dx_own, parts)
        if i == 0:
            received, mine = work
        if i == 1:
            full, new_0, new_1 = work
        back.update(zip(coming, more))
        before = (own, *moves)
    total = add(own, moves[0][: token_count + EXTRA], moves[1])
    mixed = total[:token_count].astype(BF16)
    input_grad = add(dx_own[0], moves[0][token_count + EXTRA :]).astype(BF16)
    by_expert = total[token_count:].reshape(-1)[: experts * token_count]
    by_expert = by_expert.reshape(experts, token_count)
    gate_grad = jnp.sum(jnp.where(hit, by_expert.T[:, None, :], 0.0), axis=2)

    hot = hot_slot[0]
    is_mine = hot % 2 == c
    flags = jnp.stack([hot // 2 == x, is_mine, c == 1]).astype(jnp.int32)
    def pick(piece, other):
        size = piece.shape[0] // 2
        part_own = lax.dynamic_slice_in_dim(piece, c * size, size, 0)
        part_other = lax.dynamic_slice_in_dim(other, c * size, size, 0)
        return jnp.where(is_mine, part_own, part_other)

    other_0, other_1 = grid.cross_core(new_0), grid.cross_core(new_1)
    direct_0, picked = stage(grid.cross_side(pick(new_0, other_0)), pick(new_1, other_1))
    direct_1 = grid.cross_side(picked)
    hot_copy = place_hot(0, flags, new_0, other_0, direct_0, grid.cross_core(direct_0), None)
    hot_copy, direct_1 = stage(hot_copy, direct_1)
    hot_copy = place_hot(1, flags, new_1, other_1, direct_1, grid.cross_core(direct_1), hot_copy)

    new_weights = full
    return (mixed, input_grad, gate_grad, new_weights[None], hot_copy[None])


def solution(mesh):
    return jax.shard_map(
        shards,
        mesh=mesh,
        in_specs=(
            P(BOTH, None),
            P(BOTH, None),
            P(BOTH, None),
            P(BOTH, None),
            P(BOTH, None, None),
            P(BOTH, None, None),
            P(BOTH, None, None),
            P("expert"),
        ),
        out_specs=(
            P(BOTH, None),
            P(BOTH, None),
            P(BOTH, None),
            P(BOTH, None, None),
            P(BOTH, None, None),
        ),
        check_vma=False,
    )
```
